512 devices in a mesh: seq: 64 (over z, x_hi, core), head: 8 (over x_lo, y).
Axes of the slice: x: 4 (x_hi: 2, x_lo: 2; x = x_hi * 2 + x_lo), y: 4, z: 16, core: 2. Of those that a mesh axis runs over, the one named last changes fastest.
Arguments:
- attention: bfloat16 [16, 4096, 1536], P(None, 'seq', 'head'), may hold values from -6 to 6
- encoder_skip: bfloat16 [16, 8192, 1536], P('head', 'seq'), may hold values from -6 to 6
- depth_filter: float32 [3, 1536], replicated, may hold values from -3 to 3
- point_weight: bfloat16 [1536, 1536], P('head'), may hold values from -0.15625 to 0.15625
- crop_offset: int32 [16], P('head'), may hold values from 0 to 128
- target_bins: int32 [16, 128], P('head'), may hold values from 0 to 127
- cotangent: bfloat16 [16, 8192, 1536], P('head', 'seq'), may hold values from -6 to 6
Outputs:
- target_rows: bfloat16 [16, 128, 1536], P('head', 'seq')
- attention_grad: bfloat16 [16, 4096, 1536], P('head', 'seq')
- skip_grad: bfloat16 [16, 8192, 1536], P('head', 'seq')
- filter_grad: float32 [3, 1536], replicated
The draws below stay inside these ranges and needn't reach their ends.
Inputs may be any that keep to these rules, and one draw needn't show every extreme that they name: The cropped window of sequence b starts at bin crop_offset[b]; bins of it past the end of the sequence are empty. Target j of sequence b reads bin 128 * (j // 2) + target_bins[b, j] of the cropped window.
All inputs are finite; a program needn't handle non-finite values.
Results may differ from the reference program's by a relative error of at most 0.007.
Values may be sent and summed in bfloat16 or wider, within the bound.
A program may use at most 64 MiB of HBM per device.

```python
import math
import jax
import jax.numpy as jnp
from jax import lax

D = 1536
NTD = 2
R1 = 128
L0 = 4096
L1 = 8192
B = 16
NT = 128


def place_ends(drawn, stream_key, low, high):
    extent = drawn.shape
    spot = [jax.random.randint(jax.random.fold_in(stream_key, axis), (), 0, extent[axis]) for axis in range(len(extent))]
    drawn = drawn.at[tuple(spot)].set(low)
    longest = extent.index(max(extent))
    spot[longest] = (spot[longest] + 1) % extent[longest]
    return drawn.at[tuple(spot)].set(high)


def level_of(stream_key, dims, split, least, top_value):
    def one(axis_at, shards_of):
        draws = jax.random.uniform(jax.random.fold_in(jax.random.fold_in(stream_key, 6), axis_at), (shards_of,), jnp.float32, least / len(split), top_value / len(split))
        return jnp.repeat(jnp.exp(draws), dims[axis_at] // shards_of).reshape((-1,) + (1,) * (len(dims) - axis_at - 1))

    loudness = one(*split[0])
    for cut in split[1:]:
        loudness = loudness * one(*cut)
    return loudness


def normal_values(stream_key, extent, deviation, most, cuts=(), kind=jnp.bfloat16):
    drawn = deviation * jax.random.normal(stream_key, extent, jnp.float32)
    if cuts:
        drawn = drawn * level_of(stream_key, extent, cuts, -0.22, 0.18)
    return jnp.clip(drawn, -most, most).astype(kind)


def setup_inputs(seed: int = 0) -> dict:
    arg_keys = jax.random.split(jax.random.key(seed), 8)
    return {
        "attention": normal_values(arg_keys[0], (B, L0, D), 1.0, 6.0, ((1, 64), (2, 8))),
        "encoder_skip": normal_values(arg_keys[1], (B, L1, D), 1.0, 6.0, ((0, 8), (1, 64))),
        "depth_filter": normal_values(arg_keys[2], (3, D), 0.6, 3.0, (), jnp.float32),
        "point_weight": normal_values(arg_keys[3], (D, D), D ** -0.5, 0.15625, ((0, 8),)),
        "crop_offset": place_ends(jax.random.randint(arg_keys[4], (B,), 0, R1 + 1), jax.random.fold_in(arg_keys[4], 1), 0, R1).astype(jnp.int32),
        "target_bins": place_ends(jax.random.randint(arg_keys[5], (B, NT), 0, R1), jax.random.fold_in(arg_keys[5], 1), 0, R1 - 1).astype(jnp.int32),
        "cotangent": normal_values(arg_keys[6], (B, L1, D), 1.0, 6.0, ((0, 8), (1, 64))),
    }


def gelu_slope(values):
    return 0.5 * (1.0 + lax.erf(values * 0.7071067811865476)) + values * jnp.exp(-0.5 * values * values) * 0.3989422804014327

def one_sequence(attention_row, skip_row, depth_filter, point_weight, offset, targets, cot_row):
    summed = (jnp.repeat(attention_row.astype(jnp.float32), 2, axis=0) + skip_row.astype(jnp.float32)).astype(jnp.bfloat16)
    padded = jnp.pad(summed, ((1, 1), (0, 0)))
    filtered = depth_filter[0] * padded[:-2] + depth_filter[1] * padded[1:-1] + depth_filter[2] * padded[2:]
    activated = jax.nn.gelu(filtered, approximate=False).astype(jnp.bfloat16)
    mixed_rows = jnp.dot(activated, point_weight, preferred_element_type=jnp.float32)
    block_out = (summed.astype(jnp.float32) + mixed_rows).astype(jnp.bfloat16)
    places = jnp.arange(NT, dtype=jnp.int32) // NTD * R1 + targets.astype(jnp.int32) + offset.astype(jnp.int32)
    inside = places < L1
    chosen = block_out[jnp.minimum(places, L1 - 1)]
    target_rows = jnp.where(inside[:, None], chosen, jnp.zeros_like(chosen)).astype(jnp.bfloat16)
    sources = jnp.arange(L1, dtype=jnp.int32) - offset.astype(jnp.int32)
    taken = cot_row[jnp.maximum(sources, 0)]
    grad_out = jnp.where((sources >= 0)[:, None], taken, jnp.zeros_like(taken)).astype(jnp.bfloat16)
    grad_act = jnp.dot(grad_out, point_weight.T, preferred_element_type=jnp.float32)
    grad_conv = (grad_act * gelu_slope(filtered)).astype(jnp.bfloat16)
    grad_padded = jnp.pad(grad_conv, ((1, 1), (0, 0)))
    grad_sum = grad_out.astype(jnp.float32) + depth_filter[0] * grad_padded[2:] + depth_filter[1] * grad_padded[1:-1] + depth_filter[2] * grad_padded[:-2]
    skip_grad = grad_sum.astype(jnp.bfloat16)
    attention_grad = grad_sum.reshape(L1 // 2, 2, D).sum(axis=1).astype(jnp.bfloat16)
    conv_wide = grad_conv.astype(jnp.float32)
    filter_terms = jnp.stack([lax.optimization_barrier(jnp.sum(conv_wide * padded[:-2].astype(jnp.float32), axis=0)), lax.optimization_barrier(jnp.sum(conv_wide * padded[1:-1].astype(jnp.float32), axis=0)), lax.optimization_barrier(jnp.sum(conv_wide * padded[2:].astype(jnp.float32), axis=0))])
    return (target_rows, attention_grad, skip_grad, filter_terms)

def reference(attention, encoder_skip, depth_filter, point_weight, crop_offset, target_bins, cotangent):

    def per_sequence(members):
        return one_sequence(members[0], members[1], depth_filter, point_weight, members[2], members[3], members[4])
    target_rows, attention_grad, skip_grad, filter_terms = lax.map(per_sequence, (attention, encoder_skip, crop_offset, target_bins, cotangent))
    filter_grad = lax.optimization_barrier(jnp.sum(filter_terms, axis=0)) * (1.0 / math.sqrt(B * L1))
    return (target_rows, attention_grad, skip_grad, filter_grad)
```

```python
import math

import jax
import jax.numpy as jnp
from jax import lax
from jax.experimental import pallas as pl
from jax.experimental.pallas import tpu as pltpu
from jax.sharding import PartitionSpec as P

MESH = pl.DeviceIdType.MESH
ANY = pl.BlockSpec(memory_space=pl.ANY)
VM = pl.BlockSpec(memory_space=pltpu.VMEM)
SM = pl.BlockSpec(memory_space=pltpu.SMEM)
F32 = jnp.float32
BF16 = jnp.bfloat16

D = 1536
HEADS = 8
SEQ = 64
KD = D // HEADS
ROWS = 128
HALF = 64
LOCAL = 2
TILE = 128
OWNERS = D // TILE
PLANE = 32
ZS = 16
PAD = 8
SCALE = 1.0 / math.sqrt(131072.0)


def dot(a, b):
    return jnp.dot(a, b, preferred_element_type=F32)


def dot_t(a, b):
    return lax.dot_general(a, b, (((1,), (1,)), ((), ())), preferred_element_type=F32)


def kernel(
    att,
    skip,
    filt,
    weight,
    offset,
    bins,
    cot,
    tgt_out,
    att_out,
    skip_out,
    filt_out,
    attbuf,
    skipbuf,
    wbuf,
    cotbuf,
    summed,
    slope,
    gout,
    conv,
    edge_s,
    edge_r,
    edge2_s,
    edge2_r,
    rows_s,
    rows_r,
    terms,
    plane_r,
    zsum,
    z_r,
    final,
    fin_r,
    sbf,
    abf,
    pair,
    local_sem,
    att_ss,
    att_rs,
    wy_ss,
    wy_rs,
    wx_ss,
    wx_rs,
    wz_ss,
    wz_rs,
    wc_ss,
    wc_rs,
    cot_sem,
    edge_ss,
    edge_rs,
    edge2_ss,
    edge2_rs,
    rows_sem,
    red_ss,
    red_rs,
):
    s, h = lax.axis_index("seq"), lax.axis_index("head")
    z, xh, c = s // 4, (s // 2) % 2, s % 2
    xl, y = h // 4, h % 4
    x = 2 * xh + xl
    zp = z % 2

    def at(z_, xh_, c_, xl_, y_):
        return ((z_ * 2 + xh_) * 2 + c_, xl_ * 4 + y_)

    def x_peer(by):
        other = (x + by + 4) % 4
        return at(z, other // 2, c, other % 2, y)

    def y_peer(by):
        return (s, xl * 4 + (y + by + 8) % 4)

    def z_peer(by):
        return at((z + by + 2 * ZS) % ZS, xh, c, xl, y)

    core_peer = at(z, xh, 1 - c, xl, y)
    next_dev = ((s + 1) % SEQ, h)
    prev_dev = ((s + SEQ - 1) % SEQ, h)

    def plane_dev(r):
        return at(z, (r // 8) % 2, r // 16, (r // 4) % 2, r % 4)

    my_plane = c * 16 + xh * 8 + xl * 4 + y

    def owner(t):
        return t + 16 * (t % 2)

    own_w = pltpu.make_async_copy(weight, wbuf.at[pl.ds(h * KD, KD)], local_sem.at[0])
    own_skip = pltpu.make_async_copy(skip, skipbuf, local_sem.at[1])
    own_cot = pltpu.make_async_copy(cot, cotbuf.at[:, pl.ds(ROWS, ROWS)], local_sem.at[2])
    own_att = pltpu.make_async_copy(att.at[pl.ds(LOCAL * h, LOCAL)], attbuf.at[h], local_sem.at[3])
    own_w.start()
    own_att.start()
    own_skip.start()
    own_cot.start()

    barrier = pltpu.get_barrier_semaphore()

    @pl.loop(1, PLANE)
    def _(i):
        pl.semaphore_signal(barrier, inc=1, device_id=plane_dev((my_plane + i) % PLANE), device_id_type=MESH)

    @pl.loop(1, ZS)
    def _(i):
        pl.semaphore_signal(barrier, inc=1, device_id=z_peer(i), device_id_type=MESH)

    pl.semaphore_signal(barrier, inc=1, device_id=next_dev, device_id_type=MESH)
    pl.semaphore_signal(barrier, inc=1, device_id=prev_dev, device_id_type=MESH)
    pl.semaphore_wait(barrier, PLANE - 1 + ZS - 1 + 2)

    def remote(src, dst, ss, rs, dev):
        return pltpu.make_async_remote_copy(
            src_ref=src, dst_ref=dst, send_sem=ss, recv_sem=rs, device_id=dev, device_id_type=MESH
        )

    att_copies = []
    for i in range(1, HEADS):
        to = (h + i) % HEADS
        cp = remote(
            att.at[pl.ds(LOCAL * to, LOCAL)], attbuf.at[h], att_ss.at[i - 1], att_rs.at[i - 1], (s, to)
        )
        cp.start()
        att_copies.append(cp)

    QUARTER = KD // 4

    def shard_row(xl_, d):
        return (xl_ * 4 + (y + d) % 4) * KD + c * (KD // 2)

    def piece(row, n):
        return wbuf.at[pl.ds(pl.multiple_of(row, 16), n)]

    own_half = weight.at[pl.ds(pl.multiple_of(c * (KD // 2), 16), KD // 2)]
    wy = []
    for d in (1, 3, 2):
        cp = remote(own_half, piece(h * KD + c * (KD // 2), KD // 2), wy_ss.at[d - 1], wy_rs.at[d - 1], y_peer(-d))
        cp.start()
        wy.append(cp)

    def x_copies(j):
        d = j + zp * (3 - 2 * j)
        row = shard_row(xl, d)
        return [
            remote(
                piece(row + p * QUARTER, QUARTER),
                piece(row + p * QUARTER, QUARTER),
                wx_ss.at[j, p],
                wx_rs.at[j, p],
                x_peer(1 - 2 * p),
            )
            for p in range(2)
        ]

    def x_arrived(j, p):
        d = j + zp * (3 - 2 * j)
        return piece(shard_row(1 - xl, d) + p * QUARTER, QUARTER)

    def z_arrived(j, p):
        d = j + (1 - zp) * (3 - 2 * j)
        return piece(shard_row(1 - xl, d) + p * QUARTER, QUARTER)

    core_copies = []

    def to_core(ref):
        k = len(core_copies)
        cp = remote(ref, ref, wc_ss.at[k], wc_rs.at[k], core_peer)
        cp.start()
        core_copies.append(cp)

    cot_copy = remote(cot, cotbuf.at[:, pl.ds(0, ROWS)], cot_sem.at[0], cot_sem.at[1], next_dev)
    cot_copy.start()

    own_w.wait()
    x0, x1 = x_copies(0), x_copies(1)

    @pl.when(zp == 0)
    def _():
        for cp in x0:
            cp.start()

    own_skip.wait()
    own_att.wait()
    for cp in att_copies:
        cp.wait()
    up = (
        lax.broadcasted_iota(jnp.int32, (ROWS, HALF), 0) // 2
        == lax.broadcasted_iota(jnp.int32, (ROWS, HALF), 1)
    ).astype(BF16)
    for b in range(LOCAL):
        for k in range(HEADS // 2):
            wide = jnp.concatenate([dot(up, attbuf[2 * k, b]), dot(up, attbuf[2 * k + 1, b])], axis=1)
            cols = pl.ds(2 * KD * k, 2 * KD)
            both = (wide + skipbuf[b, :, cols].astype(F32)).astype(BF16)
            sbf[pl.ds(b * ROWS, ROWS), cols] = both
            summed[b, pl.ds(PAD, ROWS), cols] = both.astype(F32)
        edge_s[0, pl.ds(b, 1), :] = summed[b, pl.ds(PAD, 1), :]
        edge_s[1, pl.ds(b, 1), :] = summed[b, pl.ds(PAD + ROWS - 1, 1), :]
    edges = [
        remote(edge_s.at[0], edge_r.at[1], edge_ss.at[0], edge_rs.at[1], prev_dev),
        remote(edge_s.at[1], edge_r.at[0], edge_ss.at[1], edge_rs.at[0], next_dev),
    ]
    for cp in edges:
        cp.start()

    for i, d in enumerate((1, 3, 2)):
        wy[i].wait_recv()
        if d == 1:

            @pl.when(zp == 0)
            def _():
                for cp in x1:
                    cp.start()

        if d == 3:

            @pl.when(zp == 1)
            def _():
                for cp in x0:
                    cp.start()

        if d == 2:

            @pl.when(zp == 1)
            def _():
                for cp in x1:
                    cp.start()

        to_core(piece(shard_row(xl, d), KD // 2))

    for cp in edges:
        cp.wait_recv()
    first, last = (s > 0).astype(F32), (s < SEQ - 1).astype(F32)
    for b in range(LOCAL):
        summed[b, pl.ds(PAD - 1, 1), :] = edge_r[0, pl.ds(b, 1), :] * first
        summed[b, pl.ds(PAD + ROWS, 1), :] = edge_r[1, pl.ds(b, 1), :] * last

    def forward(b):
        @pl.loop(0, D // TILE)
        def _(t):
            cols = pl.ds(pl.multiple_of(t * TILE, TILE), TILE)
            taps = filt[:, cols]
            v = (
                taps[0:1] * summed[b, pl.ds(PAD - 1, ROWS), cols]
                + taps[1:2] * summed[b, pl.ds(PAD, ROWS), cols]
                + taps[2:3] * summed[b, pl.ds(PAD + 1, ROWS), cols]
            )
            phi = 0.5 * (1.0 + lax.erf(v * 0.7071067811865476))
            abf[pl.ds(b * ROWS, ROWS), cols] = (v * phi).astype(BF16)
            slope[b, :, cols] = phi + v * jnp.exp(-0.5 * v * v) * 0.3989422804014327

    z_copies = [[None, None], [None, None]]
    for j in range(2):
        forward(j)
        for p in range(2):
            x0_or_1 = (x0, x1)[j]
            x0_or_1[p].wait_recv()
            ref = x_arrived(j, p)
            cp = remote(ref, ref, wz_ss.at[j, p], wz_rs.at[j, p], z_peer(1 - 2 * p))
            cp.start()
            z_copies[j][p] = cp
            to_core(ref)

    own_cot.wait()
    cot_copy.wait()
    place = lax.broadcasted_iota(jnp.int32, (ROWS, 2 * ROWS), 1)
    row = lax.broadcasted_iota(jnp.int32, (ROWS, 2 * ROWS), 0)
    for b in range(LOCAL):
        chosen = (place == row + (ROWS - offset[b])) & ((place >= ROWS) | (s > 0))
        moved = dot(chosen.astype(BF16), cotbuf[b])
        gout[pl.ds(b * ROWS, ROWS), :] = moved.astype(BF16)

    pick = lax.broadcasted_iota(jnp.int32, (16, LOCAL * ROWS), 0)
    spot = lax.broadcasted_iota(jnp.int32, (16, LOCAL * ROWS), 1)
    hit = jnp.zeros((16, LOCAL * ROWS), jnp.bool_)
    before = jnp.maximum(s - 1, 0)
    for b in range(LOCAL):
        for j in range(2):
            mine = bins[b, 2 * s + j] + offset[b]
            theirs = bins[b, 2 * before + j] + offset[b] - ROWS
            hit = hit | (
                (pick == 2 * b + j) & (spot == mine + b * ROWS) & (spot < (b + 1) * ROWS)
            )
            hit = hit | (
                (pick == 4 + 2 * b + j) & (spot == theirs + b * ROWS) & (spot >= b * ROWS) & (s > 0)
            )
    hit = hit.astype(BF16)
    act_rows = dot(hit, abf[...]).astype(BF16)
    sum_rows = dot(hit, sbf[...])

    for j in range(2):
        for p in range(2):
            z_copies[j][p].wait_recv()
            to_core(z_arrived(j, p))
    for cp in core_copies:
        cp.wait_recv()

    block_rows = (sum_rows + dot(act_rows, wbuf[...])).astype(BF16).astype(F32)
    rows_s[...] = block_rows[0:8]
    rows_copy = remote(rows_s.at[pl.ds(4, 4)], rows_r, rows_sem.at[0], rows_sem.at[1], prev_dev)
    rows_copy.start()

    for t in range(D // 256):
        cols = pl.ds(t * 256, 256)
        ga = dot_t(gout[...], wbuf[cols, :])
        sums = [0.0, 0.0, 0.0]
        for b in range(LOCAL):
            gc = (ga[b * ROWS : (b + 1) * ROWS] * slope[b, :, cols]).astype(BF16).astype(F32)
            conv[b, pl.ds(PAD, ROWS), cols] = gc
            for k in range(3):
                sums[k] = sums[k] + jnp.sum(
                    gc * summed[b, pl.ds(PAD - 1 + k, ROWS), cols], axis=0, keepdims=True
                )
        for k in range(3):
            for u in range(2):
                terms[2 * t + u, pl.ds(k, 1), :] = sums[k][:, u * TILE : (u + 1) * TILE]
    for t in range(OWNERS):
        terms[t, pl.ds(3, 1), :] = jnp.zeros((1, TILE), F32)
    for b in range(LOCAL):
        edge2_s[0, pl.ds(b, 1), :] = conv[b, pl.ds(PAD, 1), :]
        edge2_s[1, pl.ds(b, 1), :] = conv[b, pl.ds(PAD + ROWS - 1, 1), :]

    for t in range(OWNERS):
        @pl.when(my_plane != owner(t))
        def _():
            remote(
                terms.at[t], plane_r.at[my_plane], red_ss.at[0], red_rs.at[0], plane_dev(owner(t))
            ).start()

        @pl.when(my_plane == owner(t))
        def _():
            plane_r[my_plane] = terms[t]

    edges2 = [
        remote(edge2_s.at[0], edge2_r.at[1], edge2_ss.at[0], edge2_rs.at[1], prev_dev),
        remote(edge2_s.at[1], edge2_r.at[0], edge2_ss.at[1], edge2_rs.at[0], next_dev),
    ]
    for cp in edges2:
        cp.start()

    t_mine = my_plane % 16
    owns = (t_mine < OWNERS) & (my_plane // 16 == t_mine % 2)

    @pl.when(owns)
    def _():
        part = plane_r.at[pl.ds(0, PLANE - 1)]
        pltpu.make_async_copy(part, part, red_rs.at[0]).wait()
        total = plane_r[0]
        for i in range(1, PLANE):
            total = total + plane_r[i]
        zsum[...] = total
        z_r[z] = total
        for i in range(1, ZS):
            remote(zsum, z_r.at[z], red_ss.at[1], red_rs.at[1], z_peer(i)).start()

    for cp in edges2:
        cp.wait()
    for b in range(LOCAL):
        conv[b, pl.ds(PAD - 1, 1), :] = edge2_r[0, pl.ds(b, 1), :] * first
        conv[b, pl.ds(PAD + ROWS, 1), :] = edge2_r[1, pl.ds(b, 1), :] * last
    for b in range(LOCAL):

        @pl.loop(0, D // TILE)
        def _(t):
            cols = pl.ds(pl.multiple_of(t * TILE, TILE), TILE)
            taps = filt[:, cols]
            gs = (
                gout[pl.ds(b * ROWS, ROWS), cols].astype(F32)
                + taps[0:1] * conv[b, pl.ds(PAD + 1, ROWS), cols]
                + taps[1:2] * conv[b, pl.ds(PAD, ROWS), cols]
                + taps[2:3] * conv[b, pl.ds(PAD - 1, ROWS), cols]
            )
            skip_out[b, :, cols] = gs.astype(BF16)
            pair[...] = gs
            att_out[b, :, cols] = (
                pair[pl.ds(0, HALF, stride=2), :] + pair[pl.ds(1, HALF, stride=2), :]
            ).astype(BF16)

    rows_copy.wait()
    for b in range(LOCAL):
        whole = rows_s[pl.ds(2 * b, 2), :] + rows_r[pl.ds(2 * b, 2), :] * last
        tgt_out[b] = whole.astype(BF16)

    @pl.when(owns)
    def _():
        part = z_r.at[pl.ds(0, ZS - 1)]
        pltpu.make_async_copy(part, part, red_rs.at[1]).wait()
        total = z_r[0]
        for i in range(1, ZS):
            total = total + z_r[i]
        final[...] = total * SCALE
        fin_r[t_mine] = total * SCALE

        @pl.loop(1, PLANE)
        def _(i):
            remote(
                final, fin_r.at[t_mine], red_ss.at[2], red_rs.at[2], plane_dev((my_plane + i) % PLANE)
            ).start()

    @pl.when(owns)
    def _():
        part = fin_r.at[pl.ds(0, OWNERS - 1)]
        pltpu.make_async_copy(part, part, red_rs.at[2]).wait()

    @pl.when(jnp.logical_not(owns))
    def _():
        pltpu.make_async_copy(fin_r, fin_r, red_rs.at[2]).wait()

    for t in range(OWNERS):
        filt_out[:, pl.ds(t * TILE, TILE)] = fin_r[t, pl.ds(0, 3), :]

    for i in range(3):
        wy[i].wait_send()
    for cp in x0 + x1 + z_copies[0] + z_copies[1] + core_copies + edges:
        cp.wait_send()

    @pl.when(owns)
    def _():
        part = plane_r.at[pl.ds(0, OWNERS - 1)]
        pltpu.make_async_copy(part, part, red_ss.at[0]).wait()
        part = z_r.at[pl.ds(0, ZS - 1)]
        pltpu.make_async_copy(part, part, red_ss.at[1]).wait()
        part = plane_r.at[pl.ds(0, PLANE - 1)]
        pltpu.make_async_copy(part, part, red_ss.at[2]).wait()

    @pl.when(jnp.logical_not(owns))
    def _():
        part = plane_r.at[pl.ds(0, OWNERS)]
        pltpu.make_async_copy(part, part, red_ss.at[0]).wait()


def shards(attention, encoder_skip, depth_filter, point_weight, crop_offset, target_bins, cotangent):
    dma = pltpu.SemaphoreType.DMA
    wide = ROWS + 2 * PAD
    return pl.pallas_call(
        kernel,
        out_shape=(
            jax.ShapeDtypeStruct((LOCAL, 2, D), BF16),
            jax.ShapeDtypeStruct((LOCAL, HALF, D), BF16),
            jax.ShapeDtypeStruct((LOCAL, ROWS, D), BF16),
            jax.ShapeDtypeStruct((3, D), F32),
        ),
        in_specs=[ANY, ANY, VM, ANY, SM, SM, ANY],
        out_specs=(VM, VM, VM, VM),
        scratch_shapes=[
            pltpu.VMEM((HEADS, LOCAL, HALF, KD), BF16),
            pltpu.VMEM((LOCAL, ROWS, D), BF16),
            pltpu.VMEM((D, D), BF16),
            pltpu.VMEM((LOCAL, 2 * ROWS, D), BF16),
            pltpu.VMEM((LOCAL, wide, D), F32),
            pltpu.VMEM((LOCAL, ROWS, D), F32),
            pltpu.VMEM((LOCAL * ROWS, D), BF16),
            pltpu.VMEM((LOCAL, wide, D), F32),
            pltpu.VMEM((2, LOCAL, D), F32),
            pltpu.VMEM((2, LOCAL, D), F32),
            pltpu.VMEM((2, LOCAL, D), F32),
            pltpu.VMEM((2, LOCAL, D), F32),
            pltpu.VMEM((8, D), F32),
            pltpu.VMEM((4, D), F32),
            pltpu.VMEM((OWNERS, 4, TILE), F32),
            pltpu.VMEM((PLANE, 4, TILE), F32),
            pltpu.VMEM((4, TILE), F32),
            pltpu.VMEM((ZS, 4, TILE), F32),
            pltpu.VMEM((4, TILE), F32),
            pltpu.VMEM((OWNERS, 4, TILE), F32),
            pltpu.VMEM((LOCAL * ROWS, D), BF16),
            pltpu.VMEM((LOCAL * ROWS, D), BF16),
            pltpu.VMEM((ROWS, TILE), F32),
            dma((4,)),
            dma((HEADS - 1,)),
            dma((HEADS - 1,)),
            dma((3,)),
            dma((3,)),
            dma((2, 2)),
            dma((2, 2)),
            dma((2, 2)),
            dma((2, 2)),
            dma((11,)),
            dma((11,)),
            dma((2,)),
            dma((2,)),
            dma((2,)),
            dma((2,)),
            dma((2,)),
            dma((2,)),
            dma((3,)),
            dma((3,)),
        ],
        compiler_params=pltpu.CompilerParams(
            collective_id=0, has_side_effects=True, vmem_limit_bytes=48 << 20
        ),
    )(attention, encoder_skip, depth_filter, point_weight, crop_offset, target_bins, cotangent)


def solution(mesh):
    in_specs = (
        P(None, "seq", "head"),
        P("head", "seq", None),
        P(),
        P("head", None),
        P("head"),
        P("head", None),
        P("head", "seq", None),
    )
    out_specs = (P("head", "seq", None), P("head", "seq", None), P("head", "seq", None), P())
    return jax.shard_map(shards, mesh=mesh, in_specs=in_specs, out_specs=out_specs, check_vma=False)
```

```python
import math

import jax
import jax.numpy as jnp
from jax import lax
from jax.experimental import pallas as pl
from jax.experimental.pallas import tpu as pltpu
from jax.sharding import PartitionSpec as P

MESH = pl.DeviceIdType.MESH
HBM = pl.BlockSpec(memory_space=pltpu.HBM)
VM = pl.BlockSpec(memory_space=pltpu.VMEM)
F32 = jnp.float32
BF16 = jnp.bfloat16

D = 1536
HEADS = 8
SEQ = 64
KD = D // HEADS
ROWS = 128
HALF = 64
LOCAL = 2
TILE = 128
OWNERS = D // TILE
PLANE = 32
ZS = 16
PAD = 8
SCALE = 1.0 / math.sqrt(131072.0)


def dot(a, b):
    return jnp.dot(a, b, preferred_element_type=F32)


def dot_t(a, b):
    return lax.dot_general(a, b, (((1,), (1,)), ((), ())), preferred_element_type=F32)


def kernel(
    att,
    skip,
    filt_h,
    weight,
    offset_h,
    bins_h,
    cot,
    tgt_out,
    att_h,
    skip_h,
    filt_out,
    filt,
    offset,
    bins,
    attv,
    apack,
    attbuf,
    skipbuf,
    wbuf,
    cotbuf,
    summed,
    slope,
    gout,
    conv,
    edge_s,
    edge_r,
    edge2_s,
    edge2_r,
    rows_s,
    rows_r,
    terms,
    plane_r,
    zsum,
    z_r,
    final,
    fin_r,
    sbf,
    abf,
    pair,
    att_out,
    skip_out,
    local_sem,
    att_ss,
    att_rs,
    wx_ss,
    wx_rs,
    wy_ss,
    wy_rs,
    wz_ss,
    wz_rs,
    wc_ss,
    wc_rs,
    cot_sem,
    edge_ss,
    edge_rs,
    edge2_ss,
    edge2_rs,
    rows_sem,
    red_ss,
    red_rs,
    plane_in,
    z_in,
):
    s, h = lax.axis_index("seq"), lax.axis_index("head")
    z, xh, c = s // 4, (s // 2) % 2, s % 2
    xl, y = h // 4, h % 4
    x = 2 * xh + xl
    zp = z % 2

    def at(z_, xh_, c_, xl_, y_):
        return ((z_ * 2 + xh_) * 2 + c_, xl_ * 4 + y_)

    def x_peer(by):
        other = (x + by + 4) % 4
        return at(z, other // 2, c, other % 2, y)

    def y_peer(by):
        return (s, xl * 4 + (y + by + 8) % 4)

    def z_peer(by):
        return at((z + by + 2 * ZS) % ZS, xh, c, xl, y)

    core_peer = at(z, xh, 1 - c, xl, y)
    next_dev = ((s + 1) % SEQ, h)
    prev_dev = ((s + SEQ - 1) % SEQ, h)

    def plane_dev(r):
        return at(z, (r // 8) % 2, r // 16, (r // 4) % 2, r % 4)

    my_plane = c * 16 + xh * 8 + xl * 4 + y

    def owner(t):
        return t + 16 * (t % 2)

    own_w = pltpu.make_async_copy(weight, wbuf.at[pl.ds(h * KD, KD)], local_sem.at[0])
    own_skip = pltpu.make_async_copy(skip, skipbuf, local_sem.at[1])
    own_cot = pltpu.make_async_copy(cot, cotbuf.at[:, pl.ds(ROWS, ROWS)], local_sem.at[2])
    own_att = pltpu.make_async_copy(att, attv, local_sem.at[3])
    small = [
        pltpu.make_async_copy(filt_h, filt, local_sem.at[4]),
        pltpu.make_async_copy(offset_h, offset, local_sem.at[5]),
        pltpu.make_async_copy(bins_h, bins, local_sem.at[6]),
    ]
    own_att.start()
    own_w.start()
    for cp in small:
        cp.start()
    own_skip.start()
    own_cot.start()

    barrier = pltpu.get_barrier_semaphore()

    @pl.loop(1, HEADS)
    def _(i):
        pl.semaphore_signal(barrier, inc=1, device_id=(s, (h + i) % HEADS), device_id_type=MESH)

    quad = [at(z, 1 - xh, c, xl, y), core_peer, at(z, 1 - xh, 1 - c, xl, y)]
    near = quad + [x_peer(1), x_peer(-1), z_peer(1), z_peer(-1), next_dev, prev_dev]
    for dev in near:
        pl.semaphore_signal(barrier, inc=1, device_id=dev, device_id_type=MESH)
    own_att.wait()
    for i in range(HEADS):
        apack[i] = jnp.concatenate([attv[LOCAL * i], attv[LOCAL * i + 1]], axis=1)
    attbuf[h] = apack[h]
    pl.semaphore_wait(barrier, HEADS - 1 + len(near))

    def greet(sem, dev):
        pl.semaphore_signal(sem, inc=1, device_id=dev, device_id_type=MESH)

    for dev in quad:
        greet(plane_in, dev)
    for by in (1, -1):
        greet(z_in.at[0], z_peer(by))

    def remote(src, dst, ss, rs, dev):
        return pltpu.make_async_remote_copy(
            src_ref=src, dst_ref=dst, send_sem=ss, recv_sem=rs, device_id=dev, device_id_type=MESH
        )

    att_copies = []
    for i in range(1, HEADS):
        to = (h + i) % HEADS
        cp = remote(
            apack.at[to], attbuf.at[h], att_ss.at[i - 1], att_rs.at[i - 1], (s, to)
        )
        cp.start()
        att_copies.append(cp)

    quarter = KD // 4

    def piece(xl_, d, p):
        row = (xl_ * 4 + (y + d) % 4) * KD + c * (KD // 2) + p * quarter
        return wbuf.at[pl.ds(pl.multiple_of(row, 16), quarter)]

    own = weight.at[pl.ds(pl.multiple_of(c * (KD // 2) + zp * quarter, 16), quarter)]
    wy, wx, wz, core_copies = {}, {}, [], []

    def to_core(ref):
        k = len(core_copies)
        cp = remote(ref, ref, wc_ss.at[k], wc_rs.at[k], core_peer)
        cp.start()
        core_copies.append(cp)

    def to_x(d, src, dst):
        wx[d] = remote(src, dst, wx_ss.at[d], wx_rs.at[d], x_peer(1 - 2 * (d % 2)))
        wx[d].start()

    def to_z(other, d):
        k = len(wz)
        ref = piece(1 - xl if other else xl, d, zp)
        cp = remote(ref, ref, wz_ss.at[k], wz_rs.at[k], z_peer(1 - 2 * (k % 2)))
        cp.start()
        wz.append((cp, other, d))

    for d in (1, 3, 2):
        wy[d] = remote(own, piece(xl, 0, zp), wy_ss.at[d - 1], wy_rs.at[d - 1], y_peer(-d))
        wy[d].start()
    to_x(0, own, piece(xl, 0, zp))

    def from_y(d):
        wy[d].wait_recv()
        ref = piece(xl, d, zp)
        to_x(d, ref, ref)
        to_z(False, d)
        to_core(ref)

    def from_x(d):
        wx[d].wait_recv()
        to_z(True, d)
        to_core(piece(1 - xl, d, zp))

    for cp in small:
        cp.wait()
    own_skip.wait()
    for cp in att_copies:
        cp.wait_recv()
    up = (
        lax.broadcasted_iota(jnp.int32, (ROWS, HALF), 0) // 2
        == lax.broadcasted_iota(jnp.int32, (ROWS, HALF), 1)
    ).astype(BF16)
    for b in range(LOCAL):
        for k in range(HEADS // 2):
            lane = slice(b * KD, (b + 1) * KD)
            wide = jnp.concatenate([dot(up, attbuf[2 * k])[:, lane], dot(up, attbuf[2 * k + 1])[:, lane]], axis=1)
            cols = pl.ds(2 * KD * k, 2 * KD)
            both = (wide + skipbuf[b, :, cols].astype(F32)).astype(BF16)
            sbf[pl.ds(b * ROWS, ROWS), cols] = both
            summed[b, pl.ds(PAD, ROWS), cols] = both.astype(F32)
        edge_s[0, pl.ds(b, 1), :] = summed[b, pl.ds(PAD, 1), :]
        edge_s[1, pl.ds(b, 1), :] = summed[b, pl.ds(PAD + ROWS - 1, 1), :]
    edges = [
        remote(edge_s.at[0], edge_r.at[1], edge_ss.at[0], edge_rs.at[1], prev_dev),
        remote(edge_s.at[1], edge_r.at[0], edge_ss.at[1], edge_rs.at[0], next_dev),
    ]
    for cp in edges:
        cp.start()

    pl.semaphore_wait(z_in.at[0], 2)
    for by in (2, -2):
        greet(z_in.at[1], z_peer(by))
    from_y(1)
    from_y(3)
    from_x(0)
    from_y(2)
    cot_copy = remote(cot, cotbuf.at[:, pl.ds(0, ROWS)], cot_sem.at[0], cot_sem.at[1], next_dev)
    cot_copy.start()

    for cp in edges:
        cp.wait_recv()
    first, last = (s > 0).astype(F32), (s < SEQ - 1).astype(F32)
    for b in range(LOCAL):
        summed[b, pl.ds(PAD - 1, 1), :] = edge_r[0, pl.ds(b, 1), :] * first
        summed[b, pl.ds(PAD + ROWS, 1), :] = edge_r[1, pl.ds(b, 1), :] * last

    def forward(b, part):
        @pl.loop(part * D // TILE // 2, (part + 1) * D // TILE // 2)
        def _(t):
            cols = pl.ds(pl.multiple_of(t * TILE, TILE), TILE)
            taps = filt[:, cols]
            v = (
                taps[0:1] * summed[b, pl.ds(PAD - 1, ROWS), cols]
                + taps[1:2] * summed[b, pl.ds(PAD, ROWS), cols]
                + taps[2:3] * summed[b, pl.ds(PAD + 1, ROWS), cols]
            )
            phi = 0.5 * (1.0 + lax.erf(v * 0.7071067811865476))
            abf[pl.ds(b * ROWS, ROWS), cols] = (v * phi).astype(BF16)
            slope[b, :, cols] = phi + v * jnp.exp(-0.5 * v * v) * 0.3989422804014327

    forward(0, 0)
    from_x(1)
    forward(0, 1)
    from_x(3)
    forward(1, 0)
    from_x(2)
    pl.semaphore_wait(z_in.at[1], 2)
    for by in (4, -4):
        greet(z_in.at[2], z_peer(by))
    forward(1, 1)
    own_w.wait()

    own_cot.wait()
    cot_copy.wait()
    place = lax.broadcasted_iota(jnp.int32, (ROWS, 2 * ROWS), 1)
    row = lax.broadcasted_iota(jnp.int32, (ROWS, 2 * ROWS), 0)
    for b in range(LOCAL):
        chosen = (place == row + (ROWS - offset[b])) & ((place >= ROWS) | (s > 0))
        moved = dot(chosen.astype(BF16), cotbuf[b])
        gout[pl.ds(b * ROWS, ROWS), :] = moved.astype(BF16)

    pick = lax.broadcasted_iota(jnp.int32, (16, LOCAL * ROWS), 0)
    spot = lax.broadcasted_iota(jnp.int32, (16, LOCAL * ROWS), 1)
    hit = jnp.zeros((16, LOCAL * ROWS), jnp.bool_)
    before = jnp.maximum(s - 1, 0)
    for b in range(LOCAL):
        for j in range(2):
            mine = bins[b, 2 * s + j] + offset[b]
            theirs = bins[b, 2 * before + j] + offset[b] - ROWS
            hit = hit | (
                (pick == 2 * b + j) & (spot == mine + b * ROWS) & (spot < (b + 1) * ROWS)
            )
            hit = hit | (
                (pick == 4 + 2 * b + j) & (spot == theirs + b * ROWS) & (spot >= b * ROWS) & (s > 0)
            )
    hit = hit.astype(BF16)
    act_rows = dot(hit, abf[...]).astype(BF16)
    sum_rows = dot(hit, sbf[...])

    for cp, other, d in wz:
        cp.wait_recv()
        to_core(piece(1 - xl if other else xl, d, 1 - zp))
    for cp in core_copies:
        cp.wait_recv()

    block_rows = (sum_rows + dot(act_rows, wbuf[...])).astype(BF16).astype(F32)
    rows_s[...] = block_rows[0:8]
    rows_copy = remote(rows_s.at[pl.ds(4, 4)], rows_r, rows_sem.at[0], rows_sem.at[1], prev_dev)
    rows_copy.start()

    for t in range(D // 256):
        cols = pl.ds(t * 256, 256)
        ga = dot_t(gout[...], wbuf[cols, :])
        sums = [0.0, 0.0, 0.0]
        for b in range(LOCAL):
            gc = (ga[b * ROWS : (b + 1) * ROWS] * slope[b, :, cols]).astype(BF16).astype(F32)
            conv[b, pl.ds(PAD, ROWS), cols] = gc
            for k in range(3):
                sums[k] = sums[k] + jnp.sum(
                    gc * summed[b, pl.ds(PAD - 1 + k, ROWS), cols], axis=0, keepdims=True
                )
        for k in range(3):
            for u in range(2):
                terms[2 * t + u, pl.ds(k, 1), :] = sums[k][:, u * TILE : (u + 1) * TILE]
    for t in range(OWNERS):
        terms[t, pl.ds(3, 1), :] = jnp.zeros((1, TILE), F32)
    for b in range(LOCAL):
        edge2_s[0, pl.ds(b, 1), :] = conv[b, pl.ds(PAD, 1), :]
        edge2_s[1, pl.ds(b, 1), :] = conv[b, pl.ds(PAD + ROWS - 1, 1), :]

    pl.semaphore_wait(plane_in, 3)
    pl.semaphore_wait(z_in.at[2], 2)
    for t in range(OWNERS):
        @pl.when(my_plane != owner(t))
        def _():
            remote(
                terms.at[t], plane_r.at[my_plane], red_ss.at[0], red_rs.at[0], plane_dev(owner(t))
            ).start()

        @pl.when(my_plane == owner(t))
        def _():
            plane_r[my_plane] = terms[t]

    edges2 = [
        remote(edge2_s.at[0], edge2_r.at[1], edge2_ss.at[0], edge2_rs.at[1], prev_dev),
        remote(edge2_s.at[1], edge2_r.at[0], edge2_ss.at[1], edge2_rs.at[0], next_dev),
    ]
    for cp in edges2:
        cp.start()

    t_mine = my_plane % 16
    owns = (t_mine < OWNERS) & (my_plane // 16 == t_mine % 2)

    @pl.when(owns)
    def _():
        part = plane_r.at[pl.ds(0, PLANE - 1)]
        pltpu.make_async_copy(part, part, red_rs.at[0]).wait()
        total = plane_r[0]
        for i in range(1, PLANE):
            total = total + plane_r[i]
        zsum[...] = total
        z_r[z] = total
        for i in range(1, ZS):
            remote(zsum, z_r.at[z], red_ss.at[1], red_rs.at[1], z_peer(i)).start()

    for cp in edges2:
        cp.wait()
    for b in range(LOCAL):
        conv[b, pl.ds(PAD - 1, 1), :] = edge2_r[0, pl.ds(b, 1), :] * first
        conv[b, pl.ds(PAD + ROWS, 1), :] = edge2_r[1, pl.ds(b, 1), :] * last
    out_copies = []
    for b in range(LOCAL):

        @pl.loop(0, D // TILE)
        def _(t):
            cols = pl.ds(pl.multiple_of(t * TILE, TILE), TILE)
            taps = filt[:, cols]
            gs = (
                gout[pl.ds(b * ROWS, ROWS), cols].astype(F32)
                + taps[0:1] * conv[b, pl.ds(PAD + 1, ROWS), cols]
                + taps[1:2] * conv[b, pl.ds(PAD, ROWS), cols]
                + taps[2:3] * conv[b, pl.ds(PAD - 1, ROWS), cols]
            )
            skip_out[b, :, cols] = gs.astype(BF16)
            pair[...] = gs
            att_out[b, :, cols] = (
                pair[pl.ds(0, HALF, stride=2), :] + pair[pl.ds(1, HALF, stride=2), :]
            ).astype(BF16)

        for i, (src, dst) in enumerate(((skip_out, skip_h), (att_out, att_h))):
            cp = pltpu.make_async_copy(src.at[b], dst.at[b], local_sem.at[7 + 2 * b + i])
            cp.start()
            out_copies.append(cp)

    rows_copy.wait()
    for b in range(LOCAL):
        whole = rows_s[pl.ds(2 * b, 2), :] + rows_r[pl.ds(2 * b, 2), :] * last
        tgt_out[b] = whole.astype(BF16)

    @pl.when(owns)
    def _():
        part = z_r.at[pl.ds(0, ZS - 1)]
        pltpu.make_async_copy(part, part, red_rs.at[1]).wait()
        total = z_r[0]
        for i in range(1, ZS):
            total = total + z_r[i]
        final[...] = total * SCALE
        fin_r[t_mine] = total * SCALE

        @pl.loop(1, PLANE)
        def _(i):
            remote(
                final, fin_r.at[t_mine], red_ss.at[2], red_rs.at[2], plane_dev((my_plane + i) % PLANE)
            ).start()

    @pl.when(owns)
    def _():
        part = fin_r.at[pl.ds(0, OWNERS - 1)]
        pltpu.make_async_copy(part, part, red_rs.at[2]).wait()

    @pl.when(jnp.logical_not(owns))
    def _():
        pltpu.make_async_copy(fin_r, fin_r, red_rs.at[2]).wait()

    for t in range(OWNERS):
        filt_out[:, pl.ds(t * TILE, TILE)] = fin_r[t, pl.ds(0, 3), :]

    for cp in out_copies:
        cp.wait()
    for cp in att_copies + list(wx.values()) + list(wy.values()) + [w[0] for w in wz] + core_copies + edges:
        cp.wait_send()

    @pl.when(owns)
    def _():
        part = plane_r.at[pl.ds(0, OWNERS - 1)]
        pltpu.make_async_copy(part, part, red_ss.at[0]).wait()
        part = z_r.at[pl.ds(0, ZS - 1)]
        pltpu.make_async_copy(part, part, red_ss.at[1]).wait()
        part = plane_r.at[pl.ds(0, PLANE - 1)]
        pltpu.make_async_copy(part, part, red_ss.at[2]).wait()

    @pl.when(jnp.logical_not(owns))
    def _():
        part = plane_r.at[pl.ds(0, OWNERS)]
        pltpu.make_async_copy(part, part, red_ss.at[0]).wait()


def finish(a, b, c, d, a_out, b_out, c_out, d_out, av, bv, cv, dv, sem_in, sem_out):
    parts = ((c, cv, c_out), (b, bv, b_out), (d, dv, d_out), (a, av, a_out))
    ins = [pltpu.make_async_copy(x, v, sem_in.at[i]) for i, (x, v, _) in enumerate(parts)]
    outs = [pltpu.make_async_copy(v, o, sem_out.at[i]) for i, (_, v, o) in enumerate(parts)]
    for cp in ins:
        cp.start()
    for cp_in, cp_out in zip(ins, outs):
        cp_in.wait()
        cp_out.start()
    for cp in outs:
        cp.wait()


def shards(attention, encoder_skip, depth_filter, point_weight, crop_offset, target_bins, cotangent):
    dma = pltpu.SemaphoreType.DMA
    wide = ROWS + 2 * PAD
    outs = pl.pallas_call(
        kernel,
        out_shape=(
            jax.ShapeDtypeStruct((LOCAL, 2, D), BF16),
            jax.ShapeDtypeStruct((LOCAL, HALF, D), BF16),
            jax.ShapeDtypeStruct((LOCAL, ROWS, D), BF16),
            jax.ShapeDtypeStruct((3, D), F32),
        ),
        in_specs=[HBM] * 7,
        out_specs=(VM, HBM, HBM, VM),
        scratch_shapes=[
            pltpu.VMEM((3, D), F32),
            pltpu.SMEM((LOCAL,), jnp.int32),
            pltpu.SMEM((LOCAL, 128), jnp.int32),
            pltpu.VMEM((LOCAL * HEADS, HALF, KD), BF16),
            pltpu.VMEM((HEADS, HALF, LOCAL * KD), BF16),
            pltpu.VMEM((HEADS, HALF, LOCAL * KD), BF16),
            pltpu.VMEM((LOCAL, ROWS, D), BF16),
            pltpu.VMEM((D, D), BF16),
            pltpu.VMEM((LOCAL, 2 * ROWS, D), BF16),
            pltpu.VMEM((LOCAL, wide, D), F32),
            pltpu.VMEM((LOCAL, ROWS, D), F32),
            pltpu.VMEM((LOCAL * ROWS, D), BF16),
            pltpu.VMEM((LOCAL, wide, D), F32),
            pltpu.VMEM((2, LOCAL, D), F32),
            pltpu.VMEM((2, LOCAL, D), F32),
            pltpu.VMEM((2, LOCAL, D), F32),
            pltpu.VMEM((2, LOCAL, D), F32),
            pltpu.VMEM((8, D), F32),
            pltpu.VMEM((4, D), F32),
            pltpu.VMEM((OWNERS, 4, TILE), F32),
            pltpu.VMEM((PLANE, 4, TILE), F32),
            pltpu.VMEM((4, TILE), F32),
            pltpu.VMEM((ZS, 4, TILE), F32),
            pltpu.VMEM((4, TILE), F32),
            pltpu.VMEM((OWNERS, 4, TILE), F32),
            pltpu.VMEM((LOCAL * ROWS, D), BF16),
            pltpu.VMEM((LOCAL * ROWS, D), BF16),
            pltpu.VMEM((ROWS, TILE), F32),
            pltpu.VMEM((LOCAL, HALF, D), BF16),
            pltpu.VMEM((LOCAL, ROWS, D), BF16),
            dma((11,)),
            dma((HEADS - 1,)),
            dma((HEADS - 1,)),
            dma((4,)),
            dma((4,)),
            dma((3,)),
            dma((3,)),
            dma((7,)),
            dma((7,)),
            dma((14,)),
            dma((14,)),
            dma((2,)),
            dma((2,)),
            dma((2,)),
            dma((2,)),
            dma((2,)),
            dma((2,)),
            dma((3,)),
            dma((3,)),
            pltpu.SemaphoreType.REGULAR,
            pltpu.SemaphoreType.REGULAR((3,)),
        ],
        compiler_params=pltpu.CompilerParams(
            collective_id=0, has_side_effects=True, vmem_limit_bytes=60 << 20
        ),
    )(attention, encoder_skip, depth_filter, point_weight, crop_offset, target_bins, cotangent)
    return pl.pallas_call(
        finish,
        out_shape=tuple(jax.ShapeDtypeStruct(o.shape, o.dtype) for o in outs),
        in_specs=[HBM] * 4,
        out_specs=(HBM,) * 4,
        scratch_shapes=[pltpu.VMEM(o.shape, o.dtype) for o in outs] + [dma((4,)), dma((4,))],
        compiler_params=pltpu.CompilerParams(vmem_limit_bytes=60 << 20),
    )(*outs)


def solution(mesh):
    in_specs = (
        P(None, "seq", "head"),
        P("head", "seq", None),
        P(),
        P("head", None),
        P("head"),
        P("head", None),
        P("head", "seq", None),
    )
    out_specs = (P("head", "seq", None), P("head", "seq", None), P("head", "seq", None), P())
    return jax.shard_map(shards, mesh=mesh, in_specs=in_specs, out_specs=out_specs, check_vma=False)
```

```python
import math

import jax
import jax.numpy as jnp
from jax import lax
from jax.experimental import pallas as pl
from jax.experimental.pallas import tpu as pltpu
from jax.sharding import PartitionSpec as P

MESH = pl.DeviceIdType.MESH
HBM = pl.BlockSpec(memory_space=pltpu.HBM)
VM = pl.BlockSpec(memory_space=pltpu.VMEM)
F32 = jnp.float32
BF16 = jnp.bfloat16

D = 1536
HEADS = 8
SEQ = 64
KD = D // HEADS
ROWS = 128
HALF = 64
LOCAL = 2
TILE = 128
OWNERS = D // TILE
PLANE = 32
ZS = 16
PAD = 8
BYY = False
ZL = 2
COT = 0
ATT = 2
Z_SIDES = ((1, -1), (-1, 1), (1, -1), (-1, -1), (1, -1), (-1, 1), (1, -1), (-1, -1))
SCALE = 1.0 / math.sqrt(131072.0)


def dot(a, b):
    return jnp.dot(a, b, preferred_element_type=F32)


def dot_t(a, b):
    return lax.dot_general(a, b, (((1,), (1,)), ((), ())), preferred_element_type=F32)


def kernel(
    att,
    skip,
    filt_h,
    weight,
    offset_h,
    bins_h,
    cot,
    tgt_out,
    att_h,
    skip_h,
    filt_out,
    filt,
    offset,
    bins,
    attv,
    apack,
    attbuf,
    skipbuf,
    wbuf,
    cotbuf,
    summed,
    slope,
    gout,
    conv,
    edge_s,
    edge_r,
    edge2_s,
    edge2_r,
    rows_s,
    rows_r,
    terms,
    plane_r,
    zsum,
    z_r,
    final,
    fin_r,
    sbf,
    abf,
    pair,
    att_out,
    skip_out,
    local_sem,
    att_ss,
    att_rs,
    wx_ss,
    wx_rs,
    wy_ss,
    wy_rs,
    wz_ss,
    wz_rs,
    wc_ss,
    wc_rs,
    cot_sem,
    edge_ss,
    edge_rs,
    edge2_ss,
    edge2_rs,
    rows_sem,
    red_ss,
    red_rs,
    plane_in,
    z_in,
):
    s, h = lax.axis_index("seq"), lax.axis_index("head")
    z, xh, c = s // 4, (s // 2) % 2, s % 2
    xl, y = h // 4, h % 4
    x = 2 * xh + xl
    zp = z % 2

    def at(z_, xh_, c_, xl_, y_):
        return ((z_ * 2 + xh_) * 2 + c_, xl_ * 4 + y_)

    def x_peer(by):
        other = (x + by + 4) % 4
        return at(z, other // 2, c, other % 2, y)

    def y_peer(by):
        return (s, xl * 4 + (y + by + 8) % 4)

    def z_peer(by):
        return at((z + by + 2 * ZS) % ZS, xh, c, xl, y)

    core_peer = at(z, xh, 1 - c, xl, y)
    next_dev = ((s + 1) % SEQ, h)
    prev_dev = ((s + SEQ - 1) % SEQ, h)

    def plane_dev(r):
        return at(z, (r // 8) % 2, r // 16, (r // 4) % 2, r % 4)

    my_plane = c * 16 + xh * 8 + xl * 4 + y

    def owner(t):
        return t + 16 * (t % 2)

    own_w = pltpu.make_async_copy(weight, wbuf.at[pl.ds(h * KD, KD)], local_sem.at[0])
    own_skip = pltpu.make_async_copy(skip, skipbuf, local_sem.at[1])
    own_cot = pltpu.make_async_copy(cot, cotbuf.at[:, pl.ds(ROWS, ROWS)], local_sem.at[2])
    own_att = pltpu.make_async_copy(att, attv, local_sem.at[3])
    small = [
        pltpu.make_async_copy(filt_h, filt, local_sem.at[4]),
        pltpu.make_async_copy(offset_h, offset, local_sem.at[5]),
        pltpu.make_async_copy(bins_h, bins, local_sem.at[6]),
    ]
    own_att.start()
    own_w.start()
    for cp in small:
        cp.start()
    own_skip.start()
    own_cot.start()

    barrier = pltpu.get_barrier_semaphore()

    @pl.loop(1, HEADS)
    def _(i):
        pl.semaphore_signal(barrier, inc=1, device_id=(s, (h + i) % HEADS), device_id_type=MESH)

    quad = [at(z, 1 - xh, c, xl, y), core_peer, at(z, 1 - xh, 1 - c, xl, y)]
    near = quad + [x_peer(1), x_peer(-1), z_peer(1), z_peer(-1), next_dev, prev_dev]
    for dev in near:
        pl.semaphore_signal(barrier, inc=1, device_id=dev, device_id_type=MESH)
    own_att.wait()
    for i in range(HEADS):
        apack[i] = jnp.concatenate([attv[LOCAL * i], attv[LOCAL * i + 1]], axis=1)
    attbuf[h] = apack[h]
    pl.semaphore_wait(barrier, HEADS - 1 + len(near))

    def greet(sem, dev):
        pl.semaphore_signal(sem, inc=1, device_id=dev, device_id_type=MESH)

    for dev in quad:
        greet(plane_in, dev)
    for by in (1, -1):
        greet(z_in.at[0], z_peer(by))

    def remote(src, dst, ss, rs, dev):
        return pltpu.make_async_remote_copy(
            src_ref=src, dst_ref=dst, send_sem=ss, recv_sem=rs, device_id=dev, device_id_type=MESH
        )

    att_copies = []

    def start_att():
        for i in range(1, HEADS):
            to = (h + i) % HEADS
            cp = remote(
                apack.at[to], attbuf.at[h], att_ss.at[i - 1], att_rs.at[i - 1], (s, to)
            )
            cp.start()
            att_copies.append(cp)

    cot_copy = remote(cot, cotbuf.at[:, pl.ds(0, ROWS)], cot_sem.at[0], cot_sem.at[1], next_dev)

    quarter = KD // 4

    def piece(xl_, d, p, lo=0, n=KD // 4):
        row = (xl_ * 4 + (y + d) % 4) * KD + c * (KD // 2) + p * quarter + lo
        return wbuf.at[pl.ds(pl.multiple_of(row, 16), n)]

    own = weight.at[pl.ds(pl.multiple_of(c * (KD // 2) + zp * quarter, 16), quarter)]
    wy, wx, wz, core_copies, sent = {}, {}, [], [], []

    def send(src, dst, ss, rs, k, dev):
        cp = remote(src, dst, ss.at[k], rs.at[k], dev)
        cp.start()
        sent.append(cp)
        return cp

    def to_core(ref):
        k = len(core_copies)
        core_copies.append(send(ref, ref, wc_ss, wc_rs, k, core_peer))

    WHOLE, BIG, SMALL = (0, KD // 4), (0, 32), (32, 16)

    def to_x(k, side, d, part, src=None):
        dst = piece(xl, d, zp, *part)
        wx[k] = (send(dst if src is None else src, dst, wx_ss, wx_rs, k, x_peer(side)), d, part)

    busy = (0, xh, 1 - xh)[ZL]
    pair_side = 1 - 2 * xl

    def to_z(other, d, part=WHOLE):
        k = len(wz)
        calm, full = Z_SIDES[k]
        side = calm + busy * (full - calm)
        ref = piece(1 - xl if other else xl, d, zp, *part)
        wz.append((send(ref, ref, wz_ss, wz_rs, k, z_peer(side)), other, d, part))

    def to_y(k, other, d):
        dst = piece(1 - xl if other else xl, 0, zp)
        wy[k] = send(dst if other else own, dst, wy_ss, wy_rs, k, y_peer(-d))

    if ATT == 0:
        start_att()
    to_x(0, -pair_side, 0, WHOLE, own)
    to_y(0, False, 1)
    to_y(1, False, 3)
    if COT == 0:
        cot_copy.start()
    if ATT == 1:
        start_att()
    wy[0].wait_send()
    wy[1].wait_send()
    to_y(2, False, 2)
    if ATT == 2:
        start_att()
    if COT == 1:
        cot_copy.start()

    pl.semaphore_wait(z_in.at[0], 2)
    for by in (2, -2):
        greet(z_in.at[1], z_peer(by))

    def from_y(k, d):
        wy[k].wait_recv()
        to_z(False, d)
        to_core(piece(xl, d, zp))

    def from_x(k):
        cp, d, part = wx[k]
        cp.wait_recv()
        to_z(True, d, part)
        to_core(piece(1 - xl, d, zp, *part))

    def stage1():
        from_y(0, 1)
        if not BYY:
            to_x(1, pair_side, 1, WHOLE)
        from_y(1, 3)
        if not BYY:
            to_x(2, -pair_side, 3, WHOLE)
        from_x(0)
        if BYY:
            to_y(3, True, 1)
            to_y(4, True, 3)
        if COT == 2:
            cot_copy.start()

    def stage2():
        from_y(2, 2)
        to_x(3, pair_side if BYY else -pair_side, 2, BIG)
        to_x(4, -pair_side if BYY else pair_side, 2, SMALL)
        if COT == 3:
            cot_copy.start()

    def stage3(i):
        if BYY:
            wy[3 + i].wait_recv()
            to_z(True, 1 + 2 * i)
            to_core(piece(1 - xl, 1 + 2 * i, zp))
        else:
            from_x(1 + i)

    def stage4():
        from_x(3)
        from_x(4)

    for cp in small:
        cp.wait()
    own_skip.wait()
    stage1()
    pl.semaphore_wait(z_in.at[1], 2)
    for by in (4, -4):
        greet(z_in.at[2], z_peer(by))
    for cp in att_copies:
        cp.wait_recv()
    up = (
        lax.broadcasted_iota(jnp.int32, (ROWS, HALF), 0) // 2
        == lax.broadcasted_iota(jnp.int32, (ROWS, HALF), 1)
    ).astype(BF16)
    for b in range(LOCAL):
        for k in range(HEADS // 2):
            lane = slice(b * KD, (b + 1) * KD)
            wide = jnp.concatenate([dot(up, attbuf[2 * k])[:, lane], dot(up, attbuf[2 * k + 1])[:, lane]], axis=1)
            cols = pl.ds(2 * KD * k, 2 * KD)
            both = (wide + skipbuf[b, :, cols].astype(F32)).astype(BF16)
            sbf[pl.ds(b * ROWS, ROWS), cols] = both
            summed[b, pl.ds(PAD, ROWS), cols] = both.astype(F32)
        summed[b, pl.ds(PAD - 1, 1), :] = jnp.zeros((1, D), F32)
        summed[b, pl.ds(PAD + ROWS, 1), :] = jnp.zeros((1, D), F32)
        edge_s[0, pl.ds(b, 1), :] = summed[b, pl.ds(PAD, 1), :]
        edge_s[1, pl.ds(b, 1), :] = summed[b, pl.ds(PAD + ROWS - 1, 1), :]
    edges = [
        remote(edge_s.at[0], edge_r.at[1], edge_ss.at[0], edge_rs.at[1], prev_dev),
        remote(edge_s.at[1], edge_r.at[0], edge_ss.at[1], edge_rs.at[0], next_dev),
    ]
    for cp in edges:
        cp.start()

    stage2()
    def forward(b, low, n, part=0, parts=1):
        @pl.loop(part * D // TILE // parts, (part + 1) * D // TILE // parts)
        def _(t):
            cols = pl.ds(pl.multiple_of(t * TILE, TILE), TILE)
            taps = filt[:, cols]
            v = (
                taps[0:1] * summed[b, pl.ds(PAD - 1 + low, n), cols]
                + taps[1:2] * summed[b, pl.ds(PAD + low, n), cols]
                + taps[2:3] * summed[b, pl.ds(PAD + 1 + low, n), cols]
            )
            phi = 0.5 * (1.0 + lax.erf(v * 0.7071067811865476))
            abf[pl.ds(b * ROWS + low, n), cols] = (v * phi).astype(BF16)
            slope[b, pl.ds(low, n), cols] = phi + v * jnp.exp(-0.5 * v * v) * 0.3989422804014327

    forward(0, 0, ROWS, 0, 2)
    stage3(0)
    stage3(1)
    forward(0, 0, ROWS, 1, 2)
    stage4()
    forward(1, 0, ROWS)
    for cp in edges:
        cp.wait_recv()
    first, last = (s > 0).astype(F32), (s < SEQ - 1).astype(F32)
    for b in range(LOCAL):
        summed[b, pl.ds(PAD - 1, 1), :] = edge_r[0, pl.ds(b, 1), :] * first
        summed[b, pl.ds(PAD + ROWS, 1), :] = edge_r[1, pl.ds(b, 1), :] * last

    for b in range(LOCAL):
        forward(b, 0, 16)
        forward(b, ROWS - 16, 16)
    own_w.wait()

    own_cot.wait()
    cot_copy.wait()
    place = lax.broadcasted_iota(jnp.int32, (ROWS, 2 * ROWS), 1)
    row = lax.broadcasted_iota(jnp.int32, (ROWS, 2 * ROWS), 0)
    for b in range(LOCAL):
        chosen = (place == row + (ROWS - offset[b])) & ((place >= ROWS) | (s > 0))
        moved = dot(chosen.astype(BF16), cotbuf[b])
        gout[pl.ds(b * ROWS, ROWS), :] = moved.astype(BF16)

    pick = lax.broadcasted_iota(jnp.int32, (16, LOCAL * ROWS), 0)
    spot = lax.broadcasted_iota(jnp.int32, (16, LOCAL * ROWS), 1)
    hit = jnp.zeros((16, LOCAL * ROWS), jnp.bool_)
    before = jnp.maximum(s - 1, 0)
    for b in range(LOCAL):
        for j in range(2):
            mine = bins[b, 2 * s + j] + offset[b]
            theirs = bins[b, 2 * before + j] + offset[b] - ROWS
            hit = hit | (
                (pick == 2 * b + j) & (spot == mine + b * ROWS) & (spot < (b + 1) * ROWS)
            )
            hit = hit | (
                (pick == 4 + 2 * b + j) & (spot == theirs + b * ROWS) & (spot >= b * ROWS) & (s > 0)
            )
    hit = hit.astype(BF16)
    act_rows = dot(hit, abf[...]).astype(BF16)
    sum_rows = dot(hit, sbf[...])

    for cp, other, d, part in wz:
        cp.wait_recv()
        to_core(piece(1 - xl if other else xl, d, 1 - zp, *part))
    for cp in core_copies:
        cp.wait_recv()

    block_rows = (sum_rows + dot(act_rows, wbuf[...])).astype(BF16).astype(F32)
    rows_s[...] = block_rows[0:8]
    rows_copy = remote(rows_s.at[pl.ds(4, 4)], rows_r, rows_sem.at[0], rows_sem.at[1], prev_dev)
    rows_copy.start()

    for t in range(D // 256):
        cols = pl.ds(t * 256, 256)
        ga = dot_t(gout[...], wbuf[cols, :])
        sums = [0.0, 0.0, 0.0]
        for b in range(LOCAL):
            gc = (ga[b * ROWS : (b + 1) * ROWS] * slope[b, :, cols]).astype(BF16).astype(F32)
            conv[b, pl.ds(PAD, ROWS), cols] = gc
            for k in range(3):
                sums[k] = sums[k] + jnp.sum(
                    gc * summed[b, pl.ds(PAD - 1 + k, ROWS), cols], axis=0, keepdims=True
                )
        for k in range(3):
            for u in range(2):
                terms[2 * t + u, pl.ds(k, 1), :] = sums[k][:, u * TILE : (u + 1) * TILE]
    for t in range(OWNERS):
        terms[t, pl.ds(3, 1), :] = jnp.zeros((1, TILE), F32)
    for b in range(LOCAL):
        edge2_s[0, pl.ds(b, 1), :] = conv[b, pl.ds(PAD, 1), :]
        edge2_s[1, pl.ds(b, 1), :] = conv[b, pl.ds(PAD + ROWS - 1, 1), :]

    pl.semaphore_wait(plane_in, 3)
    pl.semaphore_wait(z_in.at[2], 2)
    for t in range(OWNERS):
        @pl.when(my_plane != owner(t))
        def _():
            remote(
                terms.at[t], plane_r.at[my_plane], red_ss.at[0], red_rs.at[0], plane_dev(owner(t))
            ).start()

        @pl.when(my_plane == owner(t))
        def _():
            plane_r[my_plane] = terms[t]

    edges2 = [
        remote(edge2_s.at[0], edge2_r.at[1], edge2_ss.at[0], edge2_rs.at[1], prev_dev),
        remote(edge2_s.at[1], edge2_r.at[0], edge2_ss.at[1], edge2_rs.at[0], next_dev),
    ]
    for cp in edges2:
        cp.start()

    t_mine = my_plane % 16
    owns = (t_mine < OWNERS) & (my_plane // 16 == t_mine % 2)

    @pl.when(owns)
    def _():
        part = plane_r.at[pl.ds(0, PLANE - 1)]
        pltpu.make_async_copy(part, part, red_rs.at[0]).wait()
        total = plane_r[0]
        for i in range(1, PLANE):
            total = total + plane_r[i]
        zsum[...] = total
        z_r[z] = total
        for i in range(1, ZS):
            remote(zsum, z_r.at[z], red_ss.at[1], red_rs.at[1], z_peer(i)).start()

    for cp in edges2:
        cp.wait()
    for b in range(LOCAL):
        conv[b, pl.ds(PAD - 1, 1), :] = edge2_r[0, pl.ds(b, 1), :] * first
        conv[b, pl.ds(PAD + ROWS, 1), :] = edge2_r[1, pl.ds(b, 1), :] * last
    out_copies = []
    for b in range(LOCAL):

        @pl.loop(0, D // TILE)
        def _(t):
            cols = pl.ds(pl.multiple_of(t * TILE, TILE), TILE)
            taps = filt[:, cols]
            gs = (
                gout[pl.ds(b * ROWS, ROWS), cols].astype(F32)
                + taps[0:1] * conv[b, pl.ds(PAD + 1, ROWS), cols]
                + taps[1:2] * conv[b, pl.ds(PAD, ROWS), cols]
                + taps[2:3] * conv[b, pl.ds(PAD - 1, ROWS), cols]
            )
            skip_out[b, :, cols] = gs.astype(BF16)
            pair[...] = gs
            att_out[b, :, cols] = (
                pair[pl.ds(0, HALF, stride=2), :] + pair[pl.ds(1, HALF, stride=2), :]
            ).astype(BF16)

        for i, (src, dst) in enumerate(((skip_out, skip_h), (att_out, att_h))):
            cp = pltpu.make_async_copy(src.at[b], dst.at[b], local_sem.at[7 + 2 * b + i])
            cp.start()
            out_copies.append(cp)

    rows_copy.wait()
    for b in range(LOCAL):
        whole = rows_s[pl.ds(2 * b, 2), :] + rows_r[pl.ds(2 * b, 2), :] * last
        tgt_out[b] = whole.astype(BF16)

    @pl.when(owns)
    def _():
        part = z_r.at[pl.ds(0, ZS - 1)]
        pltpu.make_async_copy(part, part, red_rs.at[1]).wait()
        total = z_r[0]
        for i in range(1, ZS):
            total = total + z_r[i]
        final[...] = total * SCALE
        fin_r[t_mine] = total * SCALE

        @pl.loop(1, PLANE)
        def _(i):
            remote(
                final, fin_r.at[t_mine], red_ss.at[2], red_rs.at[2], plane_dev((my_plane + i) % PLANE)
            ).start()

    @pl.when(owns)
    def _():
        part = fin_r.at[pl.ds(0, OWNERS - 1)]
        pltpu.make_async_copy(part, part, red_rs.at[2]).wait()

    @pl.when(jnp.logical_not(owns))
    def _():
        pltpu.make_async_copy(fin_r, fin_r, red_rs.at[2]).wait()

    for t in range(OWNERS):
        filt_out[:, pl.ds(t * TILE, TILE)] = fin_r[t, pl.ds(0, 3), :]

    for cp in out_copies:
        cp.wait()
    for cp in att_copies + [q for q in sent if q is not wy[0] and q is not wy[1]] + edges:
        cp.wait_send()

    @pl.when(owns)
    def _():
        part = plane_r.at[pl.ds(0, OWNERS - 1)]
        pltpu.make_async_copy(part, part, red_ss.at[0]).wait()
        part = z_r.at[pl.ds(0, ZS - 1)]
        pltpu.make_async_copy(part, part, red_ss.at[1]).wait()
        part = plane_r.at[pl.ds(0, PLANE - 1)]
        pltpu.make_async_copy(part, part, red_ss.at[2]).wait()

    @pl.when(jnp.logical_not(owns))
    def _():
        part = plane_r.at[pl.ds(0, OWNERS)]
        pltpu.make_async_copy(part, part, red_ss.at[0]).wait()


def finish(a, b, c, d, a_out, b_out, c_out, d_out, av, bv, cv, dv, sem_in, sem_out):
    parts = ((c, cv, c_out), (b, bv, b_out), (d, dv, d_out), (a, av, a_out))
    ins = [pltpu.make_async_copy(x, v, sem_in.at[i]) for i, (x, v, _) in enumerate(parts)]
    outs = [pltpu.make_async_copy(v, o, sem_out.at[i]) for i, (_, v, o) in enumerate(parts)]
    for cp in ins:
        cp.start()
    for cp_in, cp_out in zip(ins, outs):
        cp_in.wait()
        cp_out.start()
    for cp in outs:
        cp.wait()


def shards(attention, encoder_skip, depth_filter, point_weight, crop_offset, target_bins, cotangent):
    dma = pltpu.SemaphoreType.DMA
    wide = ROWS + 2 * PAD
    outs = pl.pallas_call(
        kernel,
        out_shape=(
            jax.ShapeDtypeStruct((LOCAL, 2, D), BF16),
            jax.ShapeDtypeStruct((LOCAL, HALF, D), BF16),
            jax.ShapeDtypeStruct((LOCAL, ROWS, D), BF16),
            jax.ShapeDtypeStruct((3, D), F32),
        ),
        in_specs=[HBM] * 7,
        out_specs=(VM, HBM, HBM, VM),
        scratch_shapes=[
            pltpu.VMEM((3, D), F32),
            pltpu.SMEM((LOCAL,), jnp.int32),
            pltpu.SMEM((LOCAL, 128), jnp.int32),
            pltpu.VMEM((LOCAL * HEADS, HALF, KD), BF16),
            pltpu.VMEM((HEADS, HALF, LOCAL * KD), BF16),
            pltpu.VMEM((HEADS, HALF, LOCAL * KD), BF16),
            pltpu.VMEM((LOCAL, ROWS, D), BF16),
            pltpu.VMEM((D, D), BF16),
            pltpu.VMEM((LOCAL, 2 * ROWS, D), BF16),
            pltpu.VMEM((LOCAL, wide, D), F32),
            pltpu.VMEM((LOCAL, ROWS, D), F32),
            pltpu.VMEM((LOCAL * ROWS, D), BF16),
            pltpu.VMEM((LOCAL, wide, D), F32),
            pltpu.VMEM((2, LOCAL, D), F32),
            pltpu.VMEM((2, LOCAL, D), F32),
            pltpu.VMEM((2, LOCAL, D), F32),
            pltpu.VMEM((2, LOCAL, D), F32),
            pltpu.VMEM((8, D), F32),
            pltpu.VMEM((4, D), F32),
            pltpu.VMEM((OWNERS, 4, TILE), F32),
            pltpu.VMEM((PLANE, 4, TILE), F32),
            pltpu.VMEM((4, TILE), F32),
            pltpu.VMEM((ZS, 4, TILE), F32),
            pltpu.VMEM((4, TILE), F32),
            pltpu.VMEM((OWNERS, 4, TILE), F32),
            pltpu.VMEM((LOCAL * ROWS, D), BF16),
            pltpu.VMEM((LOCAL * ROWS, D), BF16),
            pltpu.VMEM((ROWS, TILE), F32),
            pltpu.VMEM((LOCAL, HALF, D), BF16),
            pltpu.VMEM((LOCAL, ROWS, D), BF16),
            dma((11,)),
            dma((HEADS - 1,)),
            dma((HEADS - 1,)),
            dma((5,)),
            dma((5,)),
            dma((5,)),
            dma((5,)),
            dma((8,)),
            dma((8,)),
            dma((16,)),
            dma((16,)),
            dma((2,)),
            dma((2,)),
            dma((2,)),
            dma((2,)),
            dma((2,)),
            dma((2,)),
            dma((3,)),
            dma((3,)),
            pltpu.SemaphoreType.REGULAR,
            pltpu.SemaphoreType.REGULAR((3,)),
        ],
        compiler_params=pltpu.CompilerParams(
            collective_id=0, has_side_effects=True, vmem_limit_bytes=60 << 20
        ),
    )(attention, encoder_skip, depth_filter, point_weight, crop_offset, target_bins, cotangent)
    return pl.pallas_call(
        finish,
        out_shape=tuple(jax.ShapeDtypeStruct(o.shape, o.dtype) for o in outs),
        in_specs=[HBM] * 4,
        out_specs=(HBM,) * 4,
        scratch_shapes=[pltpu.VMEM(o.shape, o.dtype) for o in outs] + [dma((4,)), dma((4,))],
        compiler_params=pltpu.CompilerParams(vmem_limit_bytes=60 << 20),
    )(*outs)


def solution(mesh):
    in_specs = (
        P(None, "seq", "head"),
        P("head", "seq", None),
        P(),
        P("head", None),
        P("head"),
        P("head", None),
        P("head", "seq", None),
    )
    out_specs = (P("head", "seq", None), P("head", "seq", None), P("head", "seq", None), P())
    return jax.shard_map(shards, mesh=mesh, in_specs=in_specs, out_specs=out_specs, check_vma=False)
```

```python
import math

import jax
import jax.numpy as jnp
from jax import lax
from jax.experimental import pallas as pl
from jax.experimental.pallas import tpu as pltpu
from jax.sharding import PartitionSpec as P

MESH = pl.DeviceIdType.MESH
HBM = pl.BlockSpec(memory_space=pltpu.HBM)
VM = pl.BlockSpec(memory_space=pltpu.VMEM)
F32 = jnp.float32
BF16 = jnp.bfloat16

D = 1536
HEADS = 8
SEQ = 64
KD = D // HEADS
ROWS = 128
HALF = 64
LOCAL = 2
TILE = 128
OWNERS = D // TILE
PLANE = 32
ZS = 16
PAD = 8
BYY = False
ZL = 2
COT = 0
ATT = 2
Z_SIDES = ((1, -1), (-1, 1), (1, -1), (-1, -1), (1, -1), (-1, 1), (1, -1), (-1, -1))
SCALE = 1.0 / math.sqrt(131072.0)


def dot(a, b):
    return jnp.dot(a, b, preferred_element_type=F32)


def dot_t(a, b):
    return lax.dot_general(a, b, (((1,), (1,)), ((), ())), preferred_element_type=F32)


def kernel(
    att,
    skip,
    filt_h,
    weight,
    offset_h,
    bins_h,
    cot,
    tgt_out,
    att_h,
    skip_h,
    filt_out,
    filt,
    offset,
    bins,
    attv,
    apack,
    attbuf,
    skipbuf,
    wbuf,
    cotbuf,
    summed,
    slope,
    gout,
    conv,
    edge_s,
    edge_r,
    edge2_s,
    edge2_r,
    rows_s,
    rows_r,
    terms,
    plane_r,
    zsum,
    z_r,
    final,
    fin_r,
    sbf,
    abf,
    pair,
    att_out,
    skip_out,
    local_sem,
    att_ss,
    att_rs,
    wx_ss,
    wx_rs,
    wy_ss,
    wy_rs,
    wz_ss,
    wz_rs,
    wc_ss,
    wc_rs,
    cot_sem,
    edge_ss,
    edge_rs,
    edge2_ss,
    edge2_rs,
    rows_sem,
    red_ss,
    red_rs,
    plane_in,
    z_in,
):
    s, h = lax.axis_index("seq"), lax.axis_index("head")
    z, xh, c = s // 4, (s // 2) % 2, s % 2
    xl, y = h // 4, h % 4
    x = 2 * xh + xl
    zp = z % 2

    def at(z_, xh_, c_, xl_, y_):
        return ((z_ * 2 + xh_) * 2 + c_, xl_ * 4 + y_)

    def x_peer(by):
        other = (x + by + 4) % 4
        return at(z, other // 2, c, other % 2, y)

    def y_peer(by):
        return (s, xl * 4 + (y + by + 8) % 4)

    def z_peer(by):
        return at((z + by + 2 * ZS) % ZS, xh, c, xl, y)

    core_peer = at(z, xh, 1 - c, xl, y)
    next_dev = ((s + 1) % SEQ, h)
    prev_dev = ((s + SEQ - 1) % SEQ, h)

    def plane_dev(r):
        return at(z, (r // 8) % 2, r // 16, (r // 4) % 2, r % 4)

    my_plane = c * 16 + xh * 8 + xl * 4 + y

    def owner(t):
        return t + 16 * (t % 2)

    own_w = pltpu.make_async_copy(weight, wbuf.at[pl.ds(h * KD, KD)], local_sem.at[0])
    own_skip = pltpu.make_async_copy(skip, skipbuf, local_sem.at[1])
    own_cot = pltpu.make_async_copy(cot, cotbuf.at[:, pl.ds(ROWS, ROWS)], local_sem.at[2])
    own_att = pltpu.make_async_copy(att, attv, local_sem.at[3])
    small = [
        pltpu.make_async_copy(filt_h, filt, local_sem.at[4]),
        pltpu.make_async_copy(offset_h, offset, local_sem.at[5]),
        pltpu.make_async_copy(bins_h, bins, local_sem.at[6]),
    ]
    own_att.start()
    own_w.start()
    for cp in small:
        cp.start()
    own_skip.start()
    own_cot.start()

    barrier = pltpu.get_barrier_semaphore()

    @pl.loop(1, HEADS)
    def _(i):
        pl.semaphore_signal(barrier, inc=1, device_id=(s, (h + i) % HEADS), device_id_type=MESH)

    quad = [at(z, 1 - xh, c, xl, y), core_peer, at(z, 1 - xh, 1 - c, xl, y)]
    near = quad + [x_peer(1), x_peer(-1), z_peer(1), z_peer(-1), next_dev, prev_dev]
    for dev in near:
        pl.semaphore_signal(barrier, inc=1, device_id=dev, device_id_type=MESH)
    own_att.wait()
    for i in range(HEADS):
        apack[i] = jnp.concatenate([attv[LOCAL * i], attv[LOCAL * i + 1]], axis=1)
    attbuf[h] = apack[h]
    pl.semaphore_wait(barrier, HEADS - 1 + len(near))

    def greet(sem, dev):
        pl.semaphore_signal(sem, inc=1, device_id=dev, device_id_type=MESH)

    for dev in quad:
        greet(plane_in, dev)
    for by in (1, -1):
        greet(z_in.at[0], z_peer(by))

    def remote(src, dst, ss, rs, dev):
        return pltpu.make_async_remote_copy(
            src_ref=src, dst_ref=dst, send_sem=ss, recv_sem=rs, device_id=dev, device_id_type=MESH
        )

    att_copies = []

    def start_att():
        for i in range(1, HEADS):
            to = (h + i) % HEADS
            cp = remote(
                apack.at[to], attbuf.at[h], att_ss.at[i - 1], att_rs.at[i - 1], (s, to)
            )
            cp.start()
            att_copies.append(cp)

    cot_copy = remote(cot, cotbuf.at[:, pl.ds(0, ROWS)], cot_sem.at[0], cot_sem.at[1], next_dev)

    quarter = KD // 4

    def piece(xl_, d, p, lo=0, n=KD // 4):
        row = (xl_ * 4 + (y + d) % 4) * KD + c * (KD // 2) + p * quarter + lo
        return wbuf.at[pl.ds(pl.multiple_of(row, 16), n)]

    own = weight.at[pl.ds(pl.multiple_of(c * (KD // 2) + zp * quarter, 16), quarter)]
    wy, wx, wz, core_copies, sent = {}, {}, [], [], []

    def send(src, dst, ss, rs, k, dev):
        cp = remote(src, dst, ss.at[k], rs.at[k], dev)
        cp.start()
        sent.append(cp)
        return cp

    def to_core(ref):
        k = len(core_copies)
        core_copies.append(send(ref, ref, wc_ss, wc_rs, k, core_peer))

    WHOLE, BIG, SMALL = (0, KD // 4), (0, 32), (32, 16)

    def to_x(k, side, d, part, src=None):
        dst = piece(xl, d, zp, *part)
        wx[k] = (send(dst if src is None else src, dst, wx_ss, wx_rs, k, x_peer(side)), d, part)

    busy = (0, xh, 1 - xh)[ZL]
    pair_side = 1 - 2 * xl

    def to_z(other, d, part=WHOLE):
        k = len(wz)
        calm, full = Z_SIDES[k]
        side = calm + busy * (full - calm)
        ref = piece(1 - xl if other else xl, d, zp, *part)
        wz.append((send(ref, ref, wz_ss, wz_rs, k, z_peer(side)), other, d, part))

    def to_y(k, other, d):
        dst = piece(1 - xl if other else xl, 0, zp)
        wy[k] = send(dst if other else own, dst, wy_ss, wy_rs, k, y_peer(-d))

    if ATT == 0:
        start_att()
    to_x(0, -pair_side, 0, WHOLE, own)
    to_y(0, False, 1)
    to_y(1, False, 3)
    if COT == 0:
        cot_copy.start()
    if ATT == 1:
        start_att()
    wy[0].wait_send()
    wy[1].wait_send()
    to_y(2, False, 2)
    if ATT == 2:
        start_att()
    if COT == 1:
        cot_copy.start()

    pl.semaphore_wait(z_in.at[0], 2)
    for by in (2, -2):
        greet(z_in.at[1], z_peer(by))

    def from_y(k, d):
        wy[k].wait_recv()
        to_z(False, d)
        to_core(piece(xl, d, zp))

    def from_x(k):
        cp, d, part = wx[k]
        cp.wait_recv()
        to_z(True, d, part)
        to_core(piece(1 - xl, d, zp, *part))

    def stage1():
        from_y(0, 1)
        if not BYY:
            to_x(1, pair_side, 1, WHOLE)
        from_y(1, 3)
        if not BYY:
            to_x(2, -pair_side, 3, WHOLE)
        from_x(0)
        if BYY:
            to_y(3, True, 1)
            to_y(4, True, 3)
        if COT == 2:
            cot_copy.start()

    def stage2():
        from_y(2, 2)
        to_x(3, pair_side if BYY else -pair_side, 2, BIG)
        to_x(4, -pair_side if BYY else pair_side, 2, SMALL)
        if COT == 3:
            cot_copy.start()

    def stage3(i):
        if BYY:
            wy[3 + i].wait_recv()
            to_z(True, 1 + 2 * i)
            to_core(piece(1 - xl, 1 + 2 * i, zp))
        else:
            from_x(1 + i)

    def stage4():
        from_x(3)
        from_x(4)

    for cp in small:
        cp.wait()
    own_skip.wait()
    stage1()
    pl.semaphore_wait(z_in.at[1], 2)
    for by in (4, -4):
        greet(z_in.at[2], z_peer(by))
    for cp in att_copies:
        cp.wait_recv()
    up = (
        lax.broadcasted_iota(jnp.int32, (ROWS, HALF), 0) // 2
        == lax.broadcasted_iota(jnp.int32, (ROWS, HALF), 1)
    ).astype(BF16)
    for b in range(LOCAL):
        for k in range(HEADS // 2):
            lane = slice(b * KD, (b + 1) * KD)
            wide = jnp.concatenate([dot(up, attbuf[2 * k])[:, lane], dot(up, attbuf[2 * k + 1])[:, lane]], axis=1)
            cols = pl.ds(2 * KD * k, 2 * KD)
            both = (wide + skipbuf[b, :, cols].astype(F32)).astype(BF16)
            sbf[pl.ds(b * ROWS, ROWS), cols] = both
            summed[b, pl.ds(PAD, ROWS), cols] = both.astype(F32)
        summed[b, pl.ds(PAD - 1, 1), :] = jnp.zeros((1, D), F32)
        summed[b, pl.ds(PAD + ROWS, 1), :] = jnp.zeros((1, D), F32)
        edge_s[0, pl.ds(b, 1), :] = summed[b, pl.ds(PAD, 1), :]
        edge_s[1, pl.ds(b, 1), :] = summed[b, pl.ds(PAD + ROWS - 1, 1), :]
    edges = [
        remote(edge_s.at[0], edge_r.at[1], edge_ss.at[0], edge_rs.at[1], prev_dev),
        remote(edge_s.at[1], edge_r.at[0], edge_ss.at[1], edge_rs.at[0], next_dev),
    ]
    for cp in edges:
        cp.start()

    stage2()
    def forward(b, low, n, part=0, parts=1):
        @pl.loop(part * D // TILE // parts, (part + 1) * D // TILE // parts)
        def _(t):
            cols = pl.ds(pl.multiple_of(t * TILE, TILE), TILE)
            taps = filt[:, cols]
            v = (
                taps[0:1] * summed[b, pl.ds(PAD - 1 + low, n), cols]
                + taps[1:2] * summed[b, pl.ds(PAD + low, n), cols]
                + taps[2:3] * summed[b, pl.ds(PAD + 1 + low, n), cols]
            )
            phi = 0.5 * (1.0 + lax.erf(v * 0.7071067811865476))
            abf[pl.ds(b * ROWS + low, n), cols] = (v * phi).astype(BF16)
            slope[b, pl.ds(low, n), cols] = phi + v * jnp.exp(-0.5 * v * v) * 0.3989422804014327

    forward(0, 0, ROWS, 0, 2)
    stage3(0)
    stage3(1)
    forward(0, 0, ROWS, 1, 2)
    stage4()
    forward(1, 0, ROWS)
    for cp in edges:
        cp.wait_recv()
    first, last = (s > 0).astype(F32), (s < SEQ - 1).astype(F32)
    for b in range(LOCAL):
        summed[b, pl.ds(PAD - 1, 1), :] = edge_r[0, pl.ds(b, 1), :] * first
        summed[b, pl.ds(PAD + ROWS, 1), :] = edge_r[1, pl.ds(b, 1), :] * last

    for b in range(LOCAL):
        forward(b, 0, 16)
        forward(b, ROWS - 16, 16)
    own_w.wait()

    own_cot.wait()
    cot_copy.wait()
    place = lax.broadcasted_iota(jnp.int32, (ROWS, 2 * ROWS), 1)
    row = lax.broadcasted_iota(jnp.int32, (ROWS, 2 * ROWS), 0)
    for b in range(LOCAL):
        chosen = (place == row + (ROWS - offset[b])) & ((place >= ROWS) | (s > 0))
        moved = dot(chosen.astype(BF16), cotbuf[b])
        gout[pl.ds(b * ROWS, ROWS), :] = moved.astype(BF16)

    pick = lax.broadcasted_iota(jnp.int32, (16, LOCAL * ROWS), 0)
    spot = lax.broadcasted_iota(jnp.int32, (16, LOCAL * ROWS), 1)
    hit = jnp.zeros((16, LOCAL * ROWS), jnp.bool_)
    before = jnp.maximum(s - 1, 0)
    for b in range(LOCAL):
        for j in range(2):
            mine = bins[b, 2 * s + j] + offset[b]
            theirs = bins[b, 2 * before + j] + offset[b] - ROWS
            hit = hit | (
                (pick == 2 * b + j) & (spot == mine + b * ROWS) & (spot < (b + 1) * ROWS)
            )
            hit = hit | (
                (pick == 4 + 2 * b + j) & (spot == theirs + b * ROWS) & (spot >= b * ROWS) & (s > 0)
            )
    hit = hit.astype(BF16)
    act_rows = dot(hit, abf[...]).astype(BF16)
    sum_rows = dot(hit, sbf[...])

    pl.semaphore_wait(plane_in, 3)
    pl.semaphore_wait(z_in.at[2], 2)

    def block(pair_at):
        start = pl.multiple_of(pair_at * 2 * KD, TILE)
        cols = pl.ds(start, 2 * KD)
        ga = dot_t(gout[...], wbuf[cols, :])
        sums = [0.0, 0.0, 0.0]
        for b in range(LOCAL):
            gc = (ga[b * ROWS : (b + 1) * ROWS] * slope[b, :, cols]).astype(BF16).astype(F32)
            conv[b, pl.ds(PAD, ROWS), cols] = gc
            for k in range(3):
                sums[k] = sums[k] + jnp.sum(
                    gc * summed[b, pl.ds(PAD - 1 + k, ROWS), cols], axis=0, keepdims=True
                )
        for u in range(3):
            t = 3 * pair_at + u
            for k in range(3):
                terms[t, pl.ds(k, 1), :] = sums[k][:, u * TILE : (u + 1) * TILE]
            terms[t, pl.ds(3, 1), :] = jnp.zeros((1, TILE), F32)
            to = owner(t)

            @pl.when(my_plane != to)
            def _():
                remote(terms.at[t], plane_r.at[my_plane], red_ss.at[0], red_rs.at[0], plane_dev(to)).start()

            @pl.when(my_plane == to)
            def _():
                plane_r[my_plane] = terms[t]

    def from_z(*which):
        for k in which:
            cp, other, d, part = wz[k]
            cp.wait_recv()
            to_core(piece(1 - xl if other else xl, d, 1 - zp, *part))

    def from_core(*which):
        for k in which:
            core_copies[k].wait_recv()

    yh = y // 2
    from_z(0, 1, 2, 3)
    from_core(0, 1, 8, 9)
    block(2 * xl + yh)
    from_z(4, 5)
    from_core(3, 11)
    block(2 * xl + 1 - yh)
    from_z(6, 7)
    from_core(2, 4, 5, 10, 12, 13)
    block(2 * (1 - xl) + yh)
    from_core(6, 7, 14, 15)
    block(2 * (1 - xl) + 1 - yh)
    for b in range(LOCAL):
        edge2_s[0, pl.ds(b, 1), :] = conv[b, pl.ds(PAD, 1), :]
        edge2_s[1, pl.ds(b, 1), :] = conv[b, pl.ds(PAD + ROWS - 1, 1), :]

    edges2 = [
        remote(edge2_s.at[0], edge2_r.at[1], edge2_ss.at[0], edge2_rs.at[1], prev_dev),
        remote(edge2_s.at[1], edge2_r.at[0], edge2_ss.at[1], edge2_rs.at[0], next_dev),
    ]
    for cp in edges2:
        cp.start()

    block_rows = (sum_rows + dot(act_rows, wbuf[...])).astype(BF16).astype(F32)
    rows_s[...] = block_rows[0:8]
    rows_copy = remote(rows_s.at[pl.ds(4, 4)], rows_r, rows_sem.at[0], rows_sem.at[1], prev_dev)

    t_mine = my_plane % 16
    owns = (t_mine < OWNERS) & (my_plane // 16 == t_mine % 2)

    @pl.when(owns)
    def _():
        part = plane_r.at[pl.ds(0, PLANE - 1)]
        pltpu.make_async_copy(part, part, red_rs.at[0]).wait()
        total = plane_r[0]
        for i in range(1, PLANE):
            total = total + plane_r[i]
        zsum[...] = total
        z_r[z] = total
        for i in range(1, ZS):
            remote(zsum, z_r.at[z], red_ss.at[1], red_rs.at[1], z_peer(i)).start()

    rows_copy.start()

    for cp in edges2:
        cp.wait()
    for b in range(LOCAL):
        conv[b, pl.ds(PAD - 1, 1), :] = edge2_r[0, pl.ds(b, 1), :] * first
        conv[b, pl.ds(PAD + ROWS, 1), :] = edge2_r[1, pl.ds(b, 1), :] * last
    out_copies = []
    for b in range(LOCAL):

        @pl.loop(0, D // TILE)
        def _(t):
            cols = pl.ds(pl.multiple_of(t * TILE, TILE), TILE)
            taps = filt[:, cols]
            gs = (
                gout[pl.ds(b * ROWS, ROWS), cols].astype(F32)
                + taps[0:1] * conv[b, pl.ds(PAD + 1, ROWS), cols]
                + taps[1:2] * conv[b, pl.ds(PAD, ROWS), cols]
                + taps[2:3] * conv[b, pl.ds(PAD - 1, ROWS), cols]
            )
            skip_out[b, :, cols] = gs.astype(BF16)
            pair[...] = gs
            att_out[b, :, cols] = (
                pair[pl.ds(0, HALF, stride=2), :] + pair[pl.ds(1, HALF, stride=2), :]
            ).astype(BF16)

        for i, (src, dst) in enumerate(((skip_out, skip_h), (att_out, att_h))):
            cp = pltpu.make_async_copy(src.at[b], dst.at[b], local_sem.at[7 + 2 * b + i])
            cp.start()
            out_copies.append(cp)

    rows_copy.wait()
    for b in range(LOCAL):
        whole = rows_s[pl.ds(2 * b, 2), :] + rows_r[pl.ds(2 * b, 2), :] * last
        tgt_out[b] = whole.astype(BF16)

    @pl.when(owns)
    def _():
        part = z_r.at[pl.ds(0, ZS - 1)]
        pltpu.make_async_copy(part, part, red_rs.at[1]).wait()
        total = z_r[0]
        for i in range(1, ZS):
            total = total + z_r[i]
        final[...] = total * SCALE
        fin_r[t_mine] = total * SCALE

        for i in range(1, PLANE):
            remote(
                final, fin_r.at[t_mine], red_ss.at[2], red_rs.at[2], plane_dev((my_plane + i) % PLANE)
            ).start()

    @pl.when(owns)
    def _():
        part = fin_r.at[pl.ds(0, OWNERS - 1)]
        pltpu.make_async_copy(part, part, red_rs.at[2]).wait()

    @pl.when(jnp.logical_not(owns))
    def _():
        pltpu.make_async_copy(fin_r, fin_r, red_rs.at[2]).wait()

    for t in range(OWNERS):
        filt_out[:, pl.ds(t * TILE, TILE)] = fin_r[t, pl.ds(0, 3), :]

    for cp in out_copies:
        cp.wait()
    for cp in att_copies + [q for q in sent if q is not wy[0] and q is not wy[1]] + edges:
        cp.wait_send()

    @pl.when(owns)
    def _():
        part = plane_r.at[pl.ds(0, OWNERS - 1)]
        pltpu.make_async_copy(part, part, red_ss.at[0]).wait()
        part = z_r.at[pl.ds(0, ZS - 1)]
        pltpu.make_async_copy(part, part, red_ss.at[1]).wait()
        part = plane_r.at[pl.ds(0, PLANE - 1)]
        pltpu.make_async_copy(part, part, red_ss.at[2]).wait()

    @pl.when(jnp.logical_not(owns))
    def _():
        part = plane_r.at[pl.ds(0, OWNERS)]
        pltpu.make_async_copy(part, part, red_ss.at[0]).wait()


def finish(a, b, c, d, a_out, b_out, c_out, d_out, av, bv, cv, dv, sem_in, sem_out):
    parts = ((c, cv, c_out), (b, bv, b_out), (d, dv, d_out), (a, av, a_out))
    ins = [pltpu.make_async_copy(x, v, sem_in.at[i]) for i, (x, v, _) in enumerate(parts)]
    outs = [pltpu.make_async_copy(v, o, sem_out.at[i]) for i, (_, v, o) in enumerate(parts)]
    for cp in ins:
        cp.start()
    for cp_in, cp_out in zip(ins, outs):
        cp_in.wait()
        cp_out.start()
    for cp in outs:
        cp.wait()


def shards(attention, encoder_skip, depth_filter, point_weight, crop_offset, target_bins, cotangent):
    dma = pltpu.SemaphoreType.DMA
    wide = ROWS + 2 * PAD
    outs = pl.pallas_call(
        kernel,
        out_shape=(
            jax.ShapeDtypeStruct((LOCAL, 2, D), BF16),
            jax.ShapeDtypeStruct((LOCAL, HALF, D), BF16),
            jax.ShapeDtypeStruct((LOCAL, ROWS, D), BF16),
            jax.ShapeDtypeStruct((3, D), F32),
        ),
        in_specs=[HBM] * 7,
        out_specs=(VM, HBM, HBM, VM),
        scratch_shapes=[
            pltpu.VMEM((3, D), F32),
            pltpu.SMEM((LOCAL,), jnp.int32),
            pltpu.SMEM((LOCAL, 128), jnp.int32),
            pltpu.VMEM((LOCAL * HEADS, HALF, KD), BF16),
            pltpu.VMEM((HEADS, HALF, LOCAL * KD), BF16),
            pltpu.VMEM((HEADS, HALF, LOCAL * KD), BF16),
            pltpu.VMEM((LOCAL, ROWS, D), BF16),
            pltpu.VMEM((D, D), BF16),
            pltpu.VMEM((LOCAL, 2 * ROWS, D), BF16),
            pltpu.VMEM((LOCAL, wide, D), F32),
            pltpu.VMEM((LOCAL, ROWS, D), F32),
            pltpu.VMEM((LOCAL * ROWS, D), BF16),
            pltpu.VMEM((LOCAL, wide, D), F32),
            pltpu.VMEM((2, LOCAL, D), F32),
            pltpu.VMEM((2, LOCAL, D), F32),
            pltpu.VMEM((2, LOCAL, D), F32),
            pltpu.VMEM((2, LOCAL, D), F32),
            pltpu.VMEM((8, D), F32),
            pltpu.VMEM((4, D), F32),
            pltpu.VMEM((OWNERS, 4, TILE), F32),
            pltpu.VMEM((PLANE, 4, TILE), F32),
            pltpu.VMEM((4, TILE), F32),
            pltpu.VMEM((ZS, 4, TILE), F32),
            pltpu.VMEM((4, TILE), F32),
            pltpu.VMEM((OWNERS, 4, TILE), F32),
            pltpu.VMEM((LOCAL * ROWS, D), BF16),
            pltpu.VMEM((LOCAL * ROWS, D), BF16),
            pltpu.VMEM((ROWS, TILE), F32),
            pltpu.VMEM((LOCAL, HALF, D), BF16),
            pltpu.VMEM((LOCAL, ROWS, D), BF16),
            dma((11,)),
            dma((HEADS - 1,)),
            dma((HEADS - 1,)),
            dma((5,)),
            dma((5,)),
            dma((5,)),
            dma((5,)),
            dma((8,)),
            dma((8,)),
            dma((16,)),
            dma((16,)),
            dma((2,)),
            dma((2,)),
            dma((2,)),
            dma((2,)),
            dma((2,)),
            dma((2,)),
            dma((3,)),
            dma((3,)),
            pltpu.SemaphoreType.REGULAR,
            pltpu.SemaphoreType.REGULAR((3,)),
        ],
        compiler_params=pltpu.CompilerParams(
            collective_id=0, has_side_effects=True, vmem_limit_bytes=60 << 20
        ),
    )(attention, encoder_skip, depth_filter, point_weight, crop_offset, target_bins, cotangent)
    return pl.pallas_call(
        finish,
        out_shape=tuple(jax.ShapeDtypeStruct(o.shape, o.dtype) for o in outs),
        in_specs=[HBM] * 4,
        out_specs=(HBM,) * 4,
        scratch_shapes=[pltpu.VMEM(o.shape, o.dtype) for o in outs] + [dma((4,)), dma((4,))],
        compiler_params=pltpu.CompilerParams(vmem_limit_bytes=60 << 20),
    )(*outs)


def solution(mesh):
    in_specs = (
        P(None, "seq", "head"),
        P("head", "seq", None),
        P(),
        P("head", None),
        P("head"),
        P("head", None),
        P("head", "seq", None),
    )
    out_specs = (P("head", "seq", None), P("head", "seq", None), P("head", "seq", None), P())
    return jax.shard_map(shards, mesh=mesh, in_specs=in_specs, out_specs=out_specs, check_vma=False)
```

```python
import math

import jax
import jax.numpy as jnp
from jax import lax
from jax.experimental import pallas as pl
from jax.experimental.pallas import tpu as pltpu
from jax.sharding import PartitionSpec as P

MESH = pl.DeviceIdType.MESH
HBM = pl.BlockSpec(memory_space=pltpu.HBM)
VM = pl.BlockSpec(memory_space=pltpu.VMEM)
F32 = jnp.float32
BF16 = jnp.bfloat16

D = 1536
HEADS = 8
SEQ = 64
KD = D // HEADS
ROWS = 128
HALF = 64
LOCAL = 2
TILE = 128
OWNERS = D // TILE
PLANE = 32
ZS = 16
PAD = 8
BYY = False
ZL = 2
COT = 0
ATT = 2
Z_SIDES = ((1, -1), (-1, 1), (1, -1), (-1, -1), (1, 1), (-1, -1))
SCALE = 1.0 / math.sqrt(131072.0)


def dot(a, b):
    return jnp.dot(a, b, preferred_element_type=F32)


def dot_t(a, b):
    return lax.dot_general(a, b, (((1,), (1,)), ((), ())), preferred_element_type=F32)


def kernel(
    att,
    skip,
    filt_h,
    weight,
    offset_h,
    bins_h,
    cot,
    tgt_out,
    att_h,
    skip_h,
    filt_out,
    filt,
    offset,
    bins,
    attv,
    apack,
    attbuf,
    skipbuf,
    wbuf,
    cotbuf,
    summed,
    slope,
    gout,
    conv,
    edge_s,
    edge_r,
    edge2_s,
    edge2_r,
    rows_s,
    rows_r,
    terms,
    plane_r,
    zsum,
    z_r,
    final,
    fin_r,
    sbf,
    abf,
    pair,
    att_out,
    skip_out,
    local_sem,
    att_ss,
    att_rs,
    wx_ss,
    wx_rs,
    wy_ss,
    wy_rs,
    wz_ss,
    wz_rs,
    wc_ss,
    wc_rs,
    cot_sem,
    edge_ss,
    edge_rs,
    edge2_ss,
    edge2_rs,
    rows_sem,
    red_ss,
    red_rs,
    plane_in,
    z_in,
):
    s, h = lax.axis_index("seq"), lax.axis_index("head")
    z, xh, c = s // 4, (s // 2) % 2, s % 2
    xl, y = h // 4, h % 4
    x = 2 * xh + xl
    zp = z % 2

    def at(z_, xh_, c_, xl_, y_):
        return ((z_ * 2 + xh_) * 2 + c_, xl_ * 4 + y_)

    def x_peer(by):
        other = (x + by + 4) % 4
        return at(z, other // 2, c, other % 2, y)

    def y_peer(by):
        return (s, xl * 4 + (y + by + 8) % 4)

    def z_peer(by):
        return at((z + by + 2 * ZS) % ZS, xh, c, xl, y)

    core_peer = at(z, xh, 1 - c, xl, y)
    next_dev = ((s + 1) % SEQ, h)
    prev_dev = ((s + SEQ - 1) % SEQ, h)

    def plane_dev(r):
        return at(z, (r // 8) % 2, r // 16, (r // 4) % 2, r % 4)

    my_plane = c * 16 + xh * 8 + xl * 4 + y

    def owner(t):
        return t + 16 * (t % 2)

    own_w = pltpu.make_async_copy(weight, wbuf.at[pl.ds(h * KD, KD)], local_sem.at[0])
    own_skip = pltpu.make_async_copy(skip, skipbuf, local_sem.at[1])
    own_cot = pltpu.make_async_copy(cot, cotbuf.at[:, pl.ds(ROWS, ROWS)], local_sem.at[2])
    own_att = pltpu.make_async_copy(att, attv, local_sem.at[3])
    small = [
        pltpu.make_async_copy(filt_h, filt, local_sem.at[4]),
        pltpu.make_async_copy(offset_h, offset, local_sem.at[5]),
        pltpu.make_async_copy(bins_h, bins, local_sem.at[6]),
    ]
    own_att.start()
    own_w.start()
    for cp in small:
        cp.start()
    own_skip.start()
    own_cot.start()

    barrier = pltpu.get_barrier_semaphore()

    @pl.loop(1, HEADS)
    def _(i):
        pl.semaphore_signal(barrier, inc=1, device_id=(s, (h + i) % HEADS), device_id_type=MESH)

    quad = [at(z, 1 - xh, c, xl, y), core_peer, at(z, 1 - xh, 1 - c, xl, y)]
    near = quad + [x_peer(1), x_peer(-1), z_peer(1), z_peer(-1), next_dev, prev_dev]
    for dev in near:
        pl.semaphore_signal(barrier, inc=1, device_id=dev, device_id_type=MESH)
    own_att.wait()
    for i in range(HEADS):
        apack[i] = jnp.concatenate([attv[LOCAL * i], attv[LOCAL * i + 1]], axis=1)
    attbuf[h] = apack[h]
    pl.semaphore_wait(barrier, HEADS - 1 + len(near))

    def greet(sem, dev):
        pl.semaphore_signal(sem, inc=1, device_id=dev, device_id_type=MESH)

    for dev in quad:
        greet(plane_in, dev)
    for by in (1, -1):
        greet(z_in.at[0], z_peer(by))

    def remote(src, dst, ss, rs, dev):
        return pltpu.make_async_remote_copy(
            src_ref=src, dst_ref=dst, send_sem=ss, recv_sem=rs, device_id=dev, device_id_type=MESH
        )

    att_copies = []

    def start_att():
        for i in range(1, HEADS):
            to = (h + i) % HEADS
            cp = remote(
                apack.at[to], attbuf.at[h], att_ss.at[i - 1], att_rs.at[i - 1], (s, to)
            )
            cp.start()
            att_copies.append(cp)

    cot_copy = remote(cot, cotbuf.at[:, pl.ds(0, ROWS)], cot_sem.at[0], cot_sem.at[1], next_dev)

    quarter = KD // 4

    def piece(xl_, d, p, lo=0, n=KD // 4):
        row = (xl_ * 4 + (y + d) % 4) * KD + c * (KD // 2) + p * quarter + lo
        return wbuf.at[pl.ds(pl.multiple_of(row, 16), n)]

    own = weight.at[pl.ds(pl.multiple_of(c * (KD // 2) + zp * quarter, 16), quarter)]
    wy, wx, wz, core_copies, sent = {}, {}, [], [], []

    def send(src, dst, ss, rs, k, dev):
        cp = remote(src, dst, ss.at[k], rs.at[k], dev)
        cp.start()
        sent.append(cp)
        return cp

    def to_core(ref):
        k = len(core_copies)
        core_copies.append(send(ref, ref, wc_ss, wc_rs, k, core_peer))

    WHOLE, BIG, SMALL = (0, KD // 4), (0, 32), (32, 16)

    def to_x(k, side, d, part, src=None):
        dst = piece(xl, d, zp, *part)
        wx[k] = (send(dst if src is None else src, dst, wx_ss, wx_rs, k, x_peer(side)), d, part)

    busy = (0, xh, 1 - xh)[ZL]
    pair_side = 1 - 2 * xl

    def to_z(other, d, part=WHOLE):
        k = len(wz)
        calm, full = Z_SIDES[k]
        side = calm + busy * (full - calm)
        ref = piece(1 - xl if other else xl, d, zp, *part)
        wz.append((send(ref, ref, wz_ss, wz_rs, k, z_peer(side)), other, d, part))

    own_second = weight.at[pl.ds(pl.multiple_of(c * (KD // 2) + (1 - zp) * quarter, 16), quarter)]

    def second_y():
        for k, d in ((3, 1), (4, 3)):
            wy[k] = send(own_second, piece(xl, 0, 1 - zp), wy_ss, wy_rs, k, y_peer(-d))

    def to_y(k, other, d):
        dst = piece(1 - xl if other else xl, 0, zp)
        wy[k] = send(dst if other else own, dst, wy_ss, wy_rs, k, y_peer(-d))

    if ATT == 0:
        start_att()
    to_x(0, -pair_side, 0, WHOLE, own)
    to_y(0, False, 1)
    to_y(1, False, 3)
    if COT == 0:
        cot_copy.start()
    if ATT == 1:
        start_att()
    wy[0].wait_send()
    wy[1].wait_send()
    to_y(2, False, 2)
    if ATT == 3:
        second_y()
    if ATT == 2 or ATT == 3:
        start_att()
    if ATT != 3:
        second_y()
    if COT == 1:
        cot_copy.start()

    pl.semaphore_wait(z_in.at[0], 2)
    for by in (2, -2):
        greet(z_in.at[1], z_peer(by))

    def from_y(k, d):
        wy[k].wait_recv()
        if d == 2:
            to_z(False, d)
        to_core(piece(xl, d, zp))

    def from_x(k):
        cp, d, part = wx[k]
        cp.wait_recv()
        to_z(True, d, part)
        to_core(piece(1 - xl, d, zp, *part))

    def stage1():
        from_y(0, 1)
        if not BYY:
            to_x(1, pair_side, 1, WHOLE)
        from_y(1, 3)
        if not BYY:
            to_x(2, -pair_side, 3, WHOLE)
        from_x(0)
        if BYY:
            to_y(3, True, 1)
            to_y(4, True, 3)
        if COT == 2:
            cot_copy.start()

    def stage2():
        from_y(2, 2)
        to_x(3, pair_side if BYY else -pair_side, 2, BIG)
        to_x(4, -pair_side if BYY else pair_side, 2, SMALL)
        if COT == 3:
            cot_copy.start()

    def stage3(i):
        if BYY:
            wy[3 + i].wait_recv()
            to_z(True, 1 + 2 * i)
            to_core(piece(1 - xl, 1 + 2 * i, zp))
        else:
            from_x(1 + i)

    def stage4():
        from_x(3)
        from_x(4)

    for cp in small:
        cp.wait()
    own_skip.wait()
    stage1()
    pl.semaphore_wait(z_in.at[1], 2)
    for by in (4, -4):
        greet(z_in.at[2], z_peer(by))
    for cp in att_copies:
        cp.wait_recv()
    up = (
        lax.broadcasted_iota(jnp.int32, (ROWS, HALF), 0) // 2
        == lax.broadcasted_iota(jnp.int32, (ROWS, HALF), 1)
    ).astype(BF16)
    for b in range(LOCAL):
        for k in range(HEADS // 2):
            lane = slice(b * KD, (b + 1) * KD)
            wide = jnp.concatenate([dot(up, attbuf[2 * k])[:, lane], dot(up, attbuf[2 * k + 1])[:, lane]], axis=1)
            cols = pl.ds(2 * KD * k, 2 * KD)
            both = (wide + skipbuf[b, :, cols].astype(F32)).astype(BF16)
            sbf[pl.ds(b * ROWS, ROWS), cols] = both
            summed[b, pl.ds(PAD, ROWS), cols] = both.astype(F32)
        summed[b, pl.ds(PAD - 1, 1), :] = jnp.zeros((1, D), F32)
        summed[b, pl.ds(PAD + ROWS, 1), :] = jnp.zeros((1, D), F32)
        edge_s[0, pl.ds(b, 1), :] = summed[b, pl.ds(PAD, 1), :]
        edge_s[1, pl.ds(b, 1), :] = summed[b, pl.ds(PAD + ROWS - 1, 1), :]
    edges = [
        remote(edge_s.at[0], edge_r.at[1], edge_ss.at[0], edge_rs.at[1], prev_dev),
        remote(edge_s.at[1], edge_r.at[0], edge_ss.at[1], edge_rs.at[0], next_dev),
    ]
    for cp in edges:
        cp.start()

    stage2()
    def forward(b, low, n, part=0, parts=1):
        @pl.loop(part * D // TILE // parts, (part + 1) * D // TILE // parts)
        def _(t):
            cols = pl.ds(pl.multiple_of(t * TILE, TILE), TILE)
            taps = filt[:, cols]
            v = (
                taps[0:1] * summed[b, pl.ds(PAD - 1 + low, n), cols]
                + taps[1:2] * summed[b, pl.ds(PAD + low, n), cols]
                + taps[2:3] * summed[b, pl.ds(PAD + 1 + low, n), cols]
            )
            phi = 0.5 * (1.0 + lax.erf(v * 0.7071067811865476))
            abf[pl.ds(b * ROWS + low, n), cols] = (v * phi).astype(BF16)
            slope[b, pl.ds(low, n), cols] = phi + v * jnp.exp(-0.5 * v * v) * 0.3989422804014327

    forward(0, 0, ROWS, 0, 2)
    stage3(0)
    stage3(1)
    forward(0, 0, ROWS, 1, 2)
    stage4()
    forward(1, 0, ROWS)
    for cp in edges:
        cp.wait_recv()
    first, last = (s > 0).astype(F32), (s < SEQ - 1).astype(F32)
    for b in range(LOCAL):
        summed[b, pl.ds(PAD - 1, 1), :] = edge_r[0, pl.ds(b, 1), :] * first
        summed[b, pl.ds(PAD + ROWS, 1), :] = edge_r[1, pl.ds(b, 1), :] * last

    for b in range(LOCAL):
        forward(b, 0, 16)
        forward(b, ROWS - 16, 16)
    own_w.wait()

    own_cot.wait()
    cot_copy.wait()
    place = lax.broadcasted_iota(jnp.int32, (ROWS, 2 * ROWS), 1)
    row = lax.broadcasted_iota(jnp.int32, (ROWS, 2 * ROWS), 0)
    for b in range(LOCAL):
        chosen = (place == row + (ROWS - offset[b])) & ((place >= ROWS) | (s > 0))
        moved = dot(chosen.astype(BF16), cotbuf[b])
        gout[pl.ds(b * ROWS, ROWS), :] = moved.astype(BF16)

    pick = lax.broadcasted_iota(jnp.int32, (16, LOCAL * ROWS), 0)
    spot = lax.broadcasted_iota(jnp.int32, (16, LOCAL * ROWS), 1)
    hit = jnp.zeros((16, LOCAL * ROWS), jnp.bool_)
    before = jnp.maximum(s - 1, 0)
    for b in range(LOCAL):
        for j in range(2):
            mine = bins[b, 2 * s + j] + offset[b]
            theirs = bins[b, 2 * before + j] + offset[b] - ROWS
            hit = hit | (
                (pick == 2 * b + j) & (spot == mine + b * ROWS) & (spot < (b + 1) * ROWS)
            )
            hit = hit | (
                (pick == 4 + 2 * b + j) & (spot == theirs + b * ROWS) & (spot >= b * ROWS) & (s > 0)
            )
    hit = hit.astype(BF16)
    act_rows = dot(hit, abf[...]).astype(BF16)
    sum_rows = dot(hit, sbf[...])

    pl.semaphore_wait(plane_in, 3)
    pl.semaphore_wait(z_in.at[2], 2)

    def block(pair_at):
        start = pl.multiple_of(pair_at * 2 * KD, TILE)
        cols = pl.ds(start, 2 * KD)
        ga = dot_t(gout[...], wbuf[cols, :])
        sums = [0.0, 0.0, 0.0]
        for b in range(LOCAL):
            gc = (ga[b * ROWS : (b + 1) * ROWS] * slope[b, :, cols]).astype(BF16).astype(F32)
            conv[b, pl.ds(PAD, ROWS), cols] = gc
            for k in range(3):
                sums[k] = sums[k] + jnp.sum(
                    gc * summed[b, pl.ds(PAD - 1 + k, ROWS), cols], axis=0, keepdims=True
                )
        for u in range(3):
            t = 3 * pair_at + u
            for k in range(3):
                terms[t, pl.ds(k, 1), :] = sums[k][:, u * TILE : (u + 1) * TILE]
            terms[t, pl.ds(3, 1), :] = jnp.zeros((1, TILE), F32)
            to = owner(t)

            @pl.when(my_plane != to)
            def _():
                remote(terms.at[t], plane_r.at[my_plane], red_ss.at[0], red_rs.at[0], plane_dev(to)).start()

            @pl.when(my_plane == to)
            def _():
                plane_r[my_plane] = terms[t]

    def from_z(*which):
        for k in which:
            cp, other, d, part = wz[k]
            cp.wait_recv()
            to_core(piece(1 - xl if other else xl, d, 1 - zp, *part))

    def from_core(*which):
        for k in which:
            core_copies[k].wait_recv()

    yh = y // 2
    for k, d in ((3, 1), (4, 3)):
        wy[k].wait_recv()
        to_core(piece(xl, d, 1 - zp))
    from_z(0, 1)
    from_core(0, 1, 8, 9)
    block(2 * xl + yh)
    from_z(2, 3)
    from_core(3, 11)
    block(2 * xl + 1 - yh)
    from_z(4, 5)
    from_core(2, 4, 5, 10, 12, 13)
    block(2 * (1 - xl) + yh)
    from_core(6, 7, 14, 15)
    block(2 * (1 - xl) + 1 - yh)
    for b in range(LOCAL):
        edge2_s[0, pl.ds(b, 1), :] = conv[b, pl.ds(PAD, 1), :]
        edge2_s[1, pl.ds(b, 1), :] = conv[b, pl.ds(PAD + ROWS - 1, 1), :]

    edges2 = [
        remote(edge2_s.at[0], edge2_r.at[1], edge2_ss.at[0], edge2_rs.at[1], prev_dev),
        remote(edge2_s.at[1], edge2_r.at[0], edge2_ss.at[1], edge2_rs.at[0], next_dev),
    ]
    for cp in edges2:
        cp.start()

    block_rows = (sum_rows + dot(act_rows, wbuf[...])).astype(BF16).astype(F32)
    rows_s[...] = block_rows[0:8]
    rows_copy = remote(rows_s.at[pl.ds(4, 4)], rows_r, rows_sem.at[0], rows_sem.at[1], prev_dev)

    t_mine = my_plane % 16
    owns = (t_mine < OWNERS) & (my_plane // 16 == t_mine % 2)

    @pl.when(owns)
    def _():
        part = plane_r.at[pl.ds(0, PLANE - 1)]
        pltpu.make_async_copy(part, part, red_rs.at[0]).wait()
        total = plane_r[0]
        for i in range(1, PLANE):
            total = total + plane_r[i]
        zsum[...] = total
        z_r[z] = total
        for i in range(1, ZS):
            remote(zsum, z_r.at[z], red_ss.at[1], red_rs.at[1], z_peer(i)).start()

    rows_copy.start()

    for cp in edges2:
        cp.wait()
    for b in range(LOCAL):
        conv[b, pl.ds(PAD - 1, 1), :] = edge2_r[0, pl.ds(b, 1), :] * first
        conv[b, pl.ds(PAD + ROWS, 1), :] = edge2_r[1, pl.ds(b, 1), :] * last
    out_copies = []
    for b in range(LOCAL):

        @pl.loop(0, D // TILE)
        def _(t):
            cols = pl.ds(pl.multiple_of(t * TILE, TILE), TILE)
            taps = filt[:, cols]
            gs = (
                gout[pl.ds(b * ROWS, ROWS), cols].astype(F32)
                + taps[0:1] * conv[b, pl.ds(PAD + 1, ROWS), cols]
                + taps[1:2] * conv[b, pl.ds(PAD, ROWS), cols]
                + taps[2:3] * conv[b, pl.ds(PAD - 1, ROWS), cols]
            )
            skip_out[b, :, cols] = gs.astype(BF16)
            pair[...] = gs
            att_out[b, :, cols] = (
                pair[pl.ds(0, HALF, stride=2), :] + pair[pl.ds(1, HALF, stride=2), :]
            ).astype(BF16)

        for i, (src, dst) in enumerate(((skip_out, skip_h), (att_out, att_h))):
            cp = pltpu.make_async_copy(src.at[b], dst.at[b], local_sem.at[7 + 2 * b + i])
            cp.start()
            out_copies.append(cp)

    rows_copy.wait()
    for b in range(LOCAL):
        whole = rows_s[pl.ds(2 * b, 2), :] + rows_r[pl.ds(2 * b, 2), :] * last
        tgt_out[b] = whole.astype(BF16)

    @pl.when(owns)
    def _():
        part = z_r.at[pl.ds(0, ZS - 1)]
        pltpu.make_async_copy(part, part, red_rs.at[1]).wait()
        total = z_r[0]
        for i in range(1, ZS):
            total = total + z_r[i]
        final[...] = total * SCALE
        fin_r[t_mine] = total * SCALE

        for i in range(1, PLANE):
            remote(
                final, fin_r.at[t_mine], red_ss.at[2], red_rs.at[2], plane_dev((my_plane + i) % PLANE)
            ).start()

    @pl.when(owns)
    def _():
        part = fin_r.at[pl.ds(0, OWNERS - 1)]
        pltpu.make_async_copy(part, part, red_rs.at[2]).wait()

    @pl.when(jnp.logical_not(owns))
    def _():
        pltpu.make_async_copy(fin_r, fin_r, red_rs.at[2]).wait()

    for t in range(OWNERS):
        filt_out[:, pl.ds(t * TILE, TILE)] = fin_r[t, pl.ds(0, 3), :]

    for cp in out_copies:
        cp.wait()
    for cp in att_copies + [q for q in sent if q is not wy[0] and q is not wy[1]] + edges:
        cp.wait_send()

    @pl.when(owns)
    def _():
        part = plane_r.at[pl.ds(0, OWNERS - 1)]
        pltpu.make_async_copy(part, part, red_ss.at[0]).wait()
        part = z_r.at[pl.ds(0, ZS - 1)]
        pltpu.make_async_copy(part, part, red_ss.at[1]).wait()
        part = plane_r.at[pl.ds(0, PLANE - 1)]
        pltpu.make_async_copy(part, part, red_ss.at[2]).wait()

    @pl.when(jnp.logical_not(owns))
    def _():
        part = plane_r.at[pl.ds(0, OWNERS)]
        pltpu.make_async_copy(part, part, red_ss.at[0]).wait()


def finish(a, b, c, d, a_out, b_out, c_out, d_out, av, bv, cv, dv, sem_in, sem_out):
    parts = ((c, cv, c_out), (b, bv, b_out), (d, dv, d_out), (a, av, a_out))
    ins = [pltpu.make_async_copy(x, v, sem_in.at[i]) for i, (x, v, _) in enumerate(parts)]
    outs = [pltpu.make_async_copy(v, o, sem_out.at[i]) for i, (_, v, o) in enumerate(parts)]
    for cp in ins:
        cp.start()
    for cp_in, cp_out in zip(ins, outs):
        cp_in.wait()
        cp_out.start()
    for cp in outs:
        cp.wait()


def shards(attention, encoder_skip, depth_filter, point_weight, crop_offset, target_bins, cotangent):
    dma = pltpu.SemaphoreType.DMA
    wide = ROWS + 2 * PAD
    outs = pl.pallas_call(
        kernel,
        out_shape=(
            jax.ShapeDtypeStruct((LOCAL, 2, D), BF16),
            jax.ShapeDtypeStruct((LOCAL, HALF, D), BF16),
            jax.ShapeDtypeStruct((LOCAL, ROWS, D), BF16),
            jax.ShapeDtypeStruct((3, D), F32),
        ),
        in_specs=[HBM] * 7,
        out_specs=(VM, HBM, HBM, VM),
        scratch_shapes=[
            pltpu.VMEM((3, D), F32),
            pltpu.SMEM((LOCAL,), jnp.int32),
            pltpu.SMEM((LOCAL, 128), jnp.int32),
            pltpu.VMEM((LOCAL * HEADS, HALF, KD), BF16),
            pltpu.VMEM((HEADS, HALF, LOCAL * KD), BF16),
            pltpu.VMEM((HEADS, HALF, LOCAL * KD), BF16),
            pltpu.VMEM((LOCAL, ROWS, D), BF16),
            pltpu.VMEM((D, D), BF16),
            pltpu.VMEM((LOCAL, 2 * ROWS, D), BF16),
            pltpu.VMEM((LOCAL, wide, D), F32),
            pltpu.VMEM((LOCAL, ROWS, D), F32),
            pltpu.VMEM((LOCAL * ROWS, D), BF16),
            pltpu.VMEM((LOCAL, wide, D), F32),
            pltpu.VMEM((2, LOCAL, D), F32),
            pltpu.VMEM((2, LOCAL, D), F32),
            pltpu.VMEM((2, LOCAL, D), F32),
            pltpu.VMEM((2, LOCAL, D), F32),
            pltpu.VMEM((8, D), F32),
            pltpu.VMEM((4, D), F32),
            pltpu.VMEM((OWNERS, 4, TILE), F32),
            pltpu.VMEM((PLANE, 4, TILE), F32),
            pltpu.VMEM((4, TILE), F32),
            pltpu.VMEM((ZS, 4, TILE), F32),
            pltpu.VMEM((4, TILE), F32),
            pltpu.VMEM((OWNERS, 4, TILE), F32),
            pltpu.VMEM((LOCAL * ROWS, D), BF16),
            pltpu.VMEM((LOCAL * ROWS, D), BF16),
            pltpu.VMEM((ROWS, TILE), F32),
            pltpu.VMEM((LOCAL, HALF, D), BF16),
            pltpu.VMEM((LOCAL, ROWS, D), BF16),
            dma((11,)),
            dma((HEADS - 1,)),
            dma((HEADS - 1,)),
            dma((5,)),
            dma((5,)),
            dma((5,)),
            dma((5,)),
            dma((8,)),
            dma((8,)),
            dma((16,)),
            dma((16,)),
            dma((2,)),
            dma((2,)),
            dma((2,)),
            dma((2,)),
            dma((2,)),
            dma((2,)),
            dma((3,)),
            dma((3,)),
            pltpu.SemaphoreType.REGULAR,
            pltpu.SemaphoreType.REGULAR((3,)),
        ],
        compiler_params=pltpu.CompilerParams(
            collective_id=0, has_side_effects=True, vmem_limit_bytes=60 << 20
        ),
    )(attention, encoder_skip, depth_filter, point_weight, crop_offset, target_bins, cotangent)
    return pl.pallas_call(
        finish,
        out_shape=tuple(jax.ShapeDtypeStruct(o.shape, o.dtype) for o in outs),
        in_specs=[HBM] * 4,
        out_specs=(HBM,) * 4,
        scratch_shapes=[pltpu.VMEM(o.shape, o.dtype) for o in outs] + [dma((4,)), dma((4,))],
        compiler_params=pltpu.CompilerParams(vmem_limit_bytes=60 << 20),
    )(*outs)


def solution(mesh):
    in_specs = (
        P(None, "seq", "head"),
        P("head", "seq", None),
        P(),
        P("head", None),
        P("head"),
        P("head", None),
        P("head", "seq", None),
    )
    out_specs = (P("head", "seq", None), P("head", "seq", None), P("head", "seq", None), P())
    return jax.shard_map(shards, mesh=mesh, in_specs=in_specs, out_specs=out_specs, check_vma=False)
```

```python
import math

import jax
import jax.numpy as jnp
from jax import lax
from jax.experimental import pallas as pl
from jax.experimental.pallas import tpu as pltpu
from jax.sharding import PartitionSpec as P

MESH = pl.DeviceIdType.MESH
HBM = pl.BlockSpec(memory_space=pltpu.HBM)
VM = pl.BlockSpec(memory_space=pltpu.VMEM)
F32 = jnp.float32
BF16 = jnp.bfloat16

D = 1536
HEADS = 8
SEQ = 64
KD = D // HEADS
ROWS = 128
HALF = 64
LOCAL = 2
TILE = 128
OWNERS = D // TILE
PLANE = 32
ZS = 16
PAD = 8
BYY = False
ZL = 2
COT = 0
ATT = 2
Z_SIDES = ((1, -1), (-1, 1), (1, -1), (-1, -1), (1, 1), (-1, -1))
SCALE = 1.0 / math.sqrt(131072.0)


def dot(a, b):
    return jnp.dot(a, b, preferred_element_type=F32)


def dot_t(a, b):
    return lax.dot_general(a, b, (((1,), (1,)), ((), ())), preferred_element_type=F32)


def kernel(
    att,
    skip,
    filt_h,
    weight,
    offset_h,
    bins_h,
    cot,
    tgt_out,
    att_h,
    skip_h,
    filt_out,
    filt,
    offset,
    bins,
    attv,
    apack,
    attbuf,
    skipbuf,
    wbuf,
    cotbuf,
    summed,
    slope,
    gout,
    conv,
    edge_s,
    edge_r,
    edge2_s,
    edge2_r,
    rows_s,
    rows_r,
    terms,
    plane_r,
    zsum,
    z_r,
    final,
    fin_r,
    sbf,
    abf,
    pair,
    att_out,
    skip_out,
    local_sem,
    att_ss,
    att_rs,
    wx_ss,
    wx_rs,
    wy_ss,
    wy_rs,
    wz_ss,
    wz_rs,
    wc_ss,
    wc_rs,
    cot_sem,
    edge_ss,
    edge_rs,
    edge2_ss,
    edge2_rs,
    rows_sem,
    red_ss,
    red_rs,
    plane_in,
    z_in,
):
    s, h = lax.axis_index("seq"), lax.axis_index("head")
    z, xh, c = s // 4, (s // 2) % 2, s % 2
    xl, y = h // 4, h % 4
    x = 2 * xh + xl
    zp = z % 2

    def at(z_, xh_, c_, xl_, y_):
        return ((z_ * 2 + xh_) * 2 + c_, xl_ * 4 + y_)

    def x_peer(by):
        other = (x + by + 4) % 4
        return at(z, other // 2, c, other % 2, y)

    def y_peer(by):
        return (s, xl * 4 + (y + by + 8) % 4)

    def z_peer(by):
        return at((z + by + 2 * ZS) % ZS, xh, c, xl, y)

    core_peer = at(z, xh, 1 - c, xl, y)
    next_dev = ((s + 1) % SEQ, h)
    prev_dev = ((s + SEQ - 1) % SEQ, h)

    def plane_dev(r):
        return at(z, (r // 8) % 2, r // 16, (r // 4) % 2, r % 4)

    my_plane = c * 16 + xh * 8 + xl * 4 + y

    def owner(t):
        return t + 16 * (t % 2)

    own_w = pltpu.make_async_copy(weight, wbuf.at[pl.ds(h * KD, KD)], local_sem.at[0])
    own_skip = pltpu.make_async_copy(skip, skipbuf, local_sem.at[1])
    own_cot = pltpu.make_async_copy(cot, cotbuf.at[:, pl.ds(ROWS, ROWS)], local_sem.at[2])
    own_att = pltpu.make_async_copy(att, attv, local_sem.at[3])
    small = [
        pltpu.make_async_copy(filt_h, filt, local_sem.at[4]),
        pltpu.make_async_copy(offset_h, offset, local_sem.at[5]),
        pltpu.make_async_copy(bins_h, bins, local_sem.at[6]),
    ]
    own_att.start()
    own_w.start()
    for cp in small:
        cp.start()
    own_skip.start()
    own_cot.start()

    barrier = pltpu.get_barrier_semaphore()

    @pl.loop(1, HEADS)
    def _(i):
        pl.semaphore_signal(barrier, inc=1, device_id=(s, (h + i) % HEADS), device_id_type=MESH)

    quad = [at(z, 1 - xh, c, xl, y), core_peer, at(z, 1 - xh, 1 - c, xl, y)]
    near = quad + [x_peer(1), x_peer(-1), z_peer(1), z_peer(-1), next_dev, prev_dev]
    for dev in near:
        pl.semaphore_signal(barrier, inc=1, device_id=dev, device_id_type=MESH)
    own_att.wait()
    for i in range(HEADS):
        apack[i] = jnp.concatenate([attv[LOCAL * i], attv[LOCAL * i + 1]], axis=1)
    attbuf[h] = apack[h]
    pl.semaphore_wait(barrier, HEADS - 1 + len(near))

    def greet(sem, dev):
        pl.semaphore_signal(sem, inc=1, device_id=dev, device_id_type=MESH)

    for dev in quad:
        greet(plane_in, dev)
    for by in (1, -1):
        greet(z_in.at[0], z_peer(by))

    def remote(src, dst, ss, rs, dev):
        return pltpu.make_async_remote_copy(
            src_ref=src, dst_ref=dst, send_sem=ss, recv_sem=rs, device_id=dev, device_id_type=MESH
        )

    att_copies = []

    def start_att():
        for i in range(1, HEADS):
            to = (h + i) % HEADS
            cp = remote(
                apack.at[to], attbuf.at[h], att_ss.at[i - 1], att_rs.at[i - 1], (s, to)
            )
            cp.start()
            att_copies.append(cp)

    cot_copy = remote(cotbuf.at[:, pl.ds(ROWS, ROWS)], cotbuf.at[:, pl.ds(0, ROWS)], cot_sem.at[0], cot_sem.at[1], next_dev)

    quarter = KD // 4

    def piece(xl_, d, p, lo=0, n=KD // 4):
        row = (xl_ * 4 + (y + d) % 4) * KD + c * (KD // 2) + p * quarter + lo
        return wbuf.at[pl.ds(pl.multiple_of(row, 16), n)]

    own_w.wait()
    own_cot.wait()
    own = piece(xl, 0, zp)
    wy, wx, wz, core_copies, sent = {}, {}, [], [], []

    def send(src, dst, ss, rs, k, dev):
        cp = remote(src, dst, ss.at[k], rs.at[k], dev)
        cp.start()
        sent.append(cp)
        return cp

    def to_core(ref):
        k = len(core_copies)
        core_copies.append(send(ref, ref, wc_ss, wc_rs, k, core_peer))

    WHOLE, BIG, SMALL = (0, KD // 4), (0, 32), (32, 16)

    def to_x(k, side, d, part, src=None):
        dst = piece(xl, d, zp, *part)
        wx[k] = (send(dst if src is None else src, dst, wx_ss, wx_rs, k, x_peer(side)), d, part)

    busy = (0, xh, 1 - xh)[ZL]
    pair_side = 1 - 2 * xl

    def to_z(other, d, part=WHOLE):
        k = len(wz)
        calm, full = Z_SIDES[k]
        side = calm + busy * (full - calm)
        ref = piece(1 - xl if other else xl, d, zp, *part)
        wz.append((send(ref, ref, wz_ss, wz_rs, k, z_peer(side)), other, d, part))

    own_second = piece(xl, 0, 1 - zp)

    def second_y():
        for k, d in ((3, 1), (4, 3)):
            wy[k] = send(own_second, piece(xl, 0, 1 - zp), wy_ss, wy_rs, k, y_peer(-d))

    def to_y(k, other, d):
        dst = piece(1 - xl if other else xl, 0, zp)
        wy[k] = send(dst if other else own, dst, wy_ss, wy_rs, k, y_peer(-d))

    if ATT == 0:
        start_att()
    to_x(0, -pair_side, 0, WHOLE, own)
    to_y(0, False, 1)
    to_y(1, False, 3)
    if COT == 0:
        cot_copy.start()
    if ATT == 1:
        start_att()
    wy[0].wait_send()
    wy[1].wait_send()
    to_y(2, False, 2)
    if ATT == 3:
        second_y()
    if ATT == 2 or ATT == 3:
        start_att()
    if ATT != 3:
        second_y()
    if COT == 1:
        cot_copy.start()

    pl.semaphore_wait(z_in.at[0], 2)
    for by in (2, -2):
        greet(z_in.at[1], z_peer(by))

    def from_y(k, d):
        wy[k].wait_recv()
        if d == 2:
            to_z(False, d)
        to_core(piece(xl, d, zp))

    def from_x(k):
        cp, d, part = wx[k]
        cp.wait_recv()
        to_z(True, d, part)
        to_core(piece(1 - xl, d, zp, *part))

    def stage1():
        from_y(0, 1)
        if not BYY:
            to_x(1, pair_side, 1, WHOLE)
        from_y(1, 3)
        if not BYY:
            to_x(2, -pair_side, 3, WHOLE)
        from_x(0)
        if BYY:
            to_y(3, True, 1)
            to_y(4, True, 3)
        if COT == 2:
            cot_copy.start()

    def stage2():
        from_y(2, 2)
        to_x(3, pair_side if BYY else -pair_side, 2, BIG)
        to_x(4, -pair_side if BYY else pair_side, 2, SMALL)
        if COT == 3:
            cot_copy.start()

    def stage3(i):
        if BYY:
            wy[3 + i].wait_recv()
            to_z(True, 1 + 2 * i)
            to_core(piece(1 - xl, 1 + 2 * i, zp))
        else:
            from_x(1 + i)

    def stage4():
        from_x(3)
        from_x(4)

    for cp in small:
        cp.wait()
    own_skip.wait()
    stage1()
    stage2()
    pl.semaphore_wait(z_in.at[1], 2)
    for by in (4, -4):
        greet(z_in.at[2], z_peer(by))
    for cp in att_copies:
        cp.wait_recv()
    up = (
        lax.broadcasted_iota(jnp.int32, (ROWS, HALF), 0) // 2
        == lax.broadcasted_iota(jnp.int32, (ROWS, HALF), 1)
    ).astype(BF16)
    for b in range(LOCAL):
        for k in range(HEADS // 2):
            lane = slice(b * KD, (b + 1) * KD)
            wide = jnp.concatenate([dot(up, attbuf[2 * k])[:, lane], dot(up, attbuf[2 * k + 1])[:, lane]], axis=1)
            cols = pl.ds(2 * KD * k, 2 * KD)
            both = (wide + skipbuf[b, :, cols].astype(F32)).astype(BF16)
            sbf[pl.ds(b * ROWS, ROWS), cols] = both
            summed[b, pl.ds(PAD, ROWS), cols] = both.astype(F32)
        summed[b, pl.ds(PAD - 1, 1), :] = jnp.zeros((1, D), F32)
        summed[b, pl.ds(PAD + ROWS, 1), :] = jnp.zeros((1, D), F32)
        edge_s[0, pl.ds(b, 1), :] = summed[b, pl.ds(PAD, 1), :]
        edge_s[1, pl.ds(b, 1), :] = summed[b, pl.ds(PAD + ROWS - 1, 1), :]
    edges = [
        remote(edge_s.at[0], edge_r.at[1], edge_ss.at[0], edge_rs.at[1], prev_dev),
        remote(edge_s.at[1], edge_r.at[0], edge_ss.at[1], edge_rs.at[0], next_dev),
    ]
    for cp in edges:
        cp.start()

    def forward(b, low, n, part=0, parts=1):
        @pl.loop(part * D // TILE // parts, (part + 1) * D // TILE // parts)
        def _(t):
            cols = pl.ds(pl.multiple_of(t * TILE, TILE), TILE)
            taps = filt[:, cols]
            v = (
                taps[0:1] * summed[b, pl.ds(PAD - 1 + low, n), cols]
                + taps[1:2] * summed[b, pl.ds(PAD + low, n), cols]
                + taps[2:3] * summed[b, pl.ds(PAD + 1 + low, n), cols]
            )
            phi = 0.5 * (1.0 + lax.erf(v * 0.7071067811865476))
            abf[pl.ds(b * ROWS + low, n), cols] = (v * phi).astype(BF16)
            slope[b, pl.ds(low, n), cols] = phi + v * jnp.exp(-0.5 * v * v) * 0.3989422804014327

    forward(0, 0, ROWS, 0, 2)
    stage3(0)
    stage3(1)
    forward(0, 0, ROWS, 1, 2)
    stage4()
    forward(1, 0, ROWS)
    for cp in edges:
        cp.wait_recv()
    first, last = (s > 0).astype(F32), (s < SEQ - 1).astype(F32)
    for b in range(LOCAL):
        summed[b, pl.ds(PAD - 1, 1), :] = edge_r[0, pl.ds(b, 1), :] * first
        summed[b, pl.ds(PAD + ROWS, 1), :] = edge_r[1, pl.ds(b, 1), :] * last

    for b in range(LOCAL):
        forward(b, 0, 16)
        forward(b, ROWS - 16, 16)

    cot_copy.wait()
    place = lax.broadcasted_iota(jnp.int32, (ROWS, 2 * ROWS), 1)
    row = lax.broadcasted_iota(jnp.int32, (ROWS, 2 * ROWS), 0)
    for b in range(LOCAL):
        chosen = (place == row + (ROWS - offset[b])) & ((place >= ROWS) | (s > 0))
        moved = dot(chosen.astype(BF16), cotbuf[b])
        gout[pl.ds(b * ROWS, ROWS), :] = moved.astype(BF16)

    pick = lax.broadcasted_iota(jnp.int32, (16, LOCAL * ROWS), 0)
    spot = lax.broadcasted_iota(jnp.int32, (16, LOCAL * ROWS), 1)
    hit = jnp.zeros((16, LOCAL * ROWS), jnp.bool_)
    before = jnp.maximum(s - 1, 0)
    for b in range(LOCAL):
        for j in range(2):
            mine = bins[b, 2 * s + j] + offset[b]
            theirs = bins[b, 2 * before + j] + offset[b] - ROWS
            hit = hit | (
                (pick == 2 * b + j) & (spot == mine + b * ROWS) & (spot < (b + 1) * ROWS)
            )
            hit = hit | (
                (pick == 4 + 2 * b + j) & (spot == theirs + b * ROWS) & (spot >= b * ROWS) & (s > 0)
            )
    hit = hit.astype(BF16)
    act_rows = dot(hit, abf[...]).astype(BF16)
    sum_rows = dot(hit, sbf[...])

    pl.semaphore_wait(plane_in, 3)
    pl.semaphore_wait(z_in.at[2], 2)

    def block(pair_at):
        start = pl.multiple_of(pair_at * 2 * KD, TILE)
        cols = pl.ds(start, 2 * KD)
        ga = dot_t(gout[...], wbuf[cols, :])
        sums = [0.0, 0.0, 0.0]
        for b in range(LOCAL):
            gc = (ga[b * ROWS : (b + 1) * ROWS] * slope[b, :, cols]).astype(BF16).astype(F32)
            conv[b, pl.ds(PAD, ROWS), cols] = gc
            for k in range(3):
                sums[k] = sums[k] + jnp.sum(
                    gc * summed[b, pl.ds(PAD - 1 + k, ROWS), cols], axis=0, keepdims=True
                )
        for u in range(3):
            t = 3 * pair_at + u
            for k in range(3):
                terms[t, pl.ds(k, 1), :] = sums[k][:, u * TILE : (u + 1) * TILE]
            terms[t, pl.ds(3, 1), :] = jnp.zeros((1, TILE), F32)
            to = owner(t)

            @pl.when(my_plane != to)
            def _():
                remote(terms.at[t], plane_r.at[my_plane], red_ss.at[0], red_rs.at[0], plane_dev(to)).start()

            @pl.when(my_plane == to)
            def _():
                plane_r[my_plane] = terms[t]

    def from_z(*which):
        for k in which:
            cp, other, d, part = wz[k]
            cp.wait_recv()
            to_core(piece(1 - xl if other else xl, d, 1 - zp, *part))

    def from_core(*which):
        for k in which:
            core_copies[k].wait_recv()

    yh = y // 2
    for k, d in ((3, 1), (4, 3)):
        wy[k].wait_recv()
        to_core(piece(xl, d, 1 - zp))
    from_z(0, 1)
    from_core(0, 1, 8, 9)
    block(2 * xl + yh)
    from_z(2, 3)
    from_core(3, 11)
    block(2 * xl + 1 - yh)
    from_z(4, 5)
    from_core(2, 4, 5, 10, 12, 13)
    block(2 * (1 - xl) + yh)
    from_core(6, 7, 14, 15)
    block(2 * (1 - xl) + 1 - yh)
    for b in range(LOCAL):
        edge2_s[0, pl.ds(b, 1), :] = conv[b, pl.ds(PAD, 1), :]
        edge2_s[1, pl.ds(b, 1), :] = conv[b, pl.ds(PAD + ROWS - 1, 1), :]

    edges2 = [
        remote(edge2_s.at[0], edge2_r.at[1], edge2_ss.at[0], edge2_rs.at[1], prev_dev),
        remote(edge2_s.at[1], edge2_r.at[0], edge2_ss.at[1], edge2_rs.at[0], next_dev),
    ]
    for cp in edges2:
        cp.start()

    block_rows = (sum_rows + dot(act_rows, wbuf[...])).astype(BF16).astype(F32)
    rows_s[...] = block_rows[0:8]
    rows_copy = remote(rows_s.at[pl.ds(4, 4)], rows_r, rows_sem.at[0], rows_sem.at[1], prev_dev)

    far_first = sorted(
        [(dx, dy, dc) for dx in range(4) for dy in range(4) for dc in range(2) if dx or dy or dc],
        key=lambda o: -(min(o[0], 4 - o[0]) + min(o[1], 4 - o[1])),
    )
    t_mine = my_plane % 16
    owns = (t_mine < OWNERS) & (my_plane // 16 == t_mine % 2)

    @pl.when(owns)
    def _():
        part = plane_r.at[pl.ds(0, PLANE - 1)]
        pltpu.make_async_copy(part, part, red_rs.at[0]).wait()
        total = plane_r[0]
        for i in range(1, PLANE):
            total = total + plane_r[i]
        zsum[...] = total
        z_r[z] = total
        for i in sorted(range(1, ZS), key=lambda i: -min(i, ZS - i)):
            remote(zsum, z_r.at[z], red_ss.at[1], red_rs.at[1], z_peer(i)).start()

    rows_copy.start()

    for cp in edges2:
        cp.wait()
    for b in range(LOCAL):
        conv[b, pl.ds(PAD - 1, 1), :] = edge2_r[0, pl.ds(b, 1), :] * first
        conv[b, pl.ds(PAD + ROWS, 1), :] = edge2_r[1, pl.ds(b, 1), :] * last
    out_copies = []
    for b in range(LOCAL):

        @pl.loop(0, D // TILE)
        def _(t):
            cols = pl.ds(pl.multiple_of(t * TILE, TILE), TILE)
            taps = filt[:, cols]
            gs = (
                gout[pl.ds(b * ROWS, ROWS), cols].astype(F32)
                + taps[0:1] * conv[b, pl.ds(PAD + 1, ROWS), cols]
                + taps[1:2] * conv[b, pl.ds(PAD, ROWS), cols]
                + taps[2:3] * conv[b, pl.ds(PAD - 1, ROWS), cols]
            )
            skip_out[b, :, cols] = gs.astype(BF16)
            pair[...] = gs
            att_out[b, :, cols] = (
                pair[pl.ds(0, HALF, stride=2), :] + pair[pl.ds(1, HALF, stride=2), :]
            ).astype(BF16)

        for i, (src, dst) in enumerate(((skip_out, skip_h), (att_out, att_h))):
            cp = pltpu.make_async_copy(src.at[b], dst.at[b], local_sem.at[7 + 2 * b + i])
            cp.start()
            out_copies.append(cp)

    rows_copy.wait()
    for b in range(LOCAL):
        whole = rows_s[pl.ds(2 * b, 2), :] + rows_r[pl.ds(2 * b, 2), :] * last
        tgt_out[b] = whole.astype(BF16)

    for cp in out_copies:
        cp.wait()
    for cp in att_copies + [q for q in sent if q is not wy[0] and q is not wy[1]] + edges:
        cp.wait_send()

    @pl.when(owns)
    def _():
        part = plane_r.at[pl.ds(0, OWNERS - 1)]
        pltpu.make_async_copy(part, part, red_ss.at[0]).wait()
        part = z_r.at[pl.ds(0, ZS - 1)]
        pltpu.make_async_copy(part, part, red_ss.at[1]).wait()

    @pl.when(jnp.logical_not(owns))
    def _():
        part = plane_r.at[pl.ds(0, OWNERS)]
        pltpu.make_async_copy(part, part, red_ss.at[0]).wait()

    @pl.when(owns)
    def _():
        part = z_r.at[pl.ds(0, ZS - 1)]
        pltpu.make_async_copy(part, part, red_rs.at[1]).wait()
        total = z_r[0]
        for i in range(1, ZS):
            total = total + z_r[i]
        final[...] = total * SCALE
        fin_r[t_mine] = total * SCALE

        for dx, dy, dc in far_first:
            other = (x + dx) % 4
            to = at(z, other // 2, 1 - c if dc else c, other % 2, (y + dy) % 4)
            remote(final, fin_r.at[t_mine], red_ss.at[2], red_rs.at[2], to).start()

    @pl.when(owns)
    def _():
        part = fin_r.at[pl.ds(0, OWNERS - 1)]
        pltpu.make_async_copy(part, part, red_rs.at[2]).wait()

    @pl.when(jnp.logical_not(owns))
    def _():
        pltpu.make_async_copy(fin_r, fin_r, red_rs.at[2]).wait()

    for t in range(OWNERS):
        filt_out[:, pl.ds(t * TILE, TILE)] = fin_r[t, pl.ds(0, 3), :]

    @pl.when(owns)
    def _():
        part = plane_r.at[pl.ds(0, PLANE - 1)]
        pltpu.make_async_copy(part, part, red_ss.at[2]).wait()


def finish(a, b, c, d, a_out, b_out, c_out, d_out, av, bv, cv, dv, sem_in, sem_out):
    parts = [(c.at[i], cv.at[i], c_out.at[i]) for i in range(LOCAL)]
    parts += [(b.at[i], bv.at[i], b_out.at[i]) for i in range(LOCAL)]
    parts += [(d, dv, d_out), (a, av, a_out)]
    ins = [pltpu.make_async_copy(x, v, sem_in.at[i]) for i, (x, v, _) in enumerate(parts)]
    outs = [pltpu.make_async_copy(v, o, sem_out.at[i]) for i, (_, v, o) in enumerate(parts)]
    for cp in ins:
        cp.start()
    for cp_in, cp_out in zip(ins, outs):
        cp_in.wait()
        cp_out.start()
    for cp in outs:
        cp.wait()


def shards(attention, encoder_skip, depth_filter, point_weight, crop_offset, target_bins, cotangent):
    dma = pltpu.SemaphoreType.DMA
    wide = ROWS + 2 * PAD
    outs = pl.pallas_call(
        kernel,
        out_shape=(
            jax.ShapeDtypeStruct((LOCAL, 2, D), BF16),
            jax.ShapeDtypeStruct((LOCAL, HALF, D), BF16),
            jax.ShapeDtypeStruct((LOCAL, ROWS, D), BF16),
            jax.ShapeDtypeStruct((3, D), F32),
        ),
        in_specs=[HBM] * 7,
        out_specs=(VM, HBM, HBM, VM),
        scratch_shapes=[
            pltpu.VMEM((3, D), F32),
            pltpu.SMEM((LOCAL,), jnp.int32),
            pltpu.SMEM((LOCAL, 128), jnp.int32),
            pltpu.VMEM((LOCAL * HEADS, HALF, KD), BF16),
            pltpu.VMEM((HEADS, HALF, LOCAL * KD), BF16),
            pltpu.VMEM((HEADS, HALF, LOCAL * KD), BF16),
            pltpu.VMEM((LOCAL, ROWS, D), BF16),
            pltpu.VMEM((D, D), BF16),
            pltpu.VMEM((LOCAL, 2 * ROWS, D), BF16),
            pltpu.VMEM((LOCAL, wide, D), F32),
            pltpu.VMEM((LOCAL, ROWS, D), F32),
            pltpu.VMEM((LOCAL * ROWS, D), BF16),
            pltpu.VMEM((LOCAL, wide, D), F32),
            pltpu.VMEM((2, LOCAL, D), F32),
            pltpu.VMEM((2, LOCAL, D), F32),
            pltpu.VMEM((2, LOCAL, D), F32),
            pltpu.VMEM((2, LOCAL, D), F32),
            pltpu.VMEM((8, D), F32),
            pltpu.VMEM((4, D), F32),
            pltpu.VMEM((OWNERS, 4, TILE), F32),
            pltpu.VMEM((PLANE, 4, TILE), F32),
            pltpu.VMEM((4, TILE), F32),
            pltpu.VMEM((ZS, 4, TILE), F32),
            pltpu.VMEM((4, TILE), F32),
            pltpu.VMEM((OWNERS, 4, TILE), F32),
            pltpu.VMEM((LOCAL * ROWS, D), BF16),
            pltpu.VMEM((LOCAL * ROWS, D), BF16),
            pltpu.VMEM((ROWS, TILE), F32),
            pltpu.VMEM((LOCAL, HALF, D), BF16),
            pltpu.VMEM((LOCAL, ROWS, D), BF16),
            dma((11,)),
            dma((HEADS - 1,)),
            dma((HEADS - 1,)),
            dma((5,)),
            dma((5,)),
            dma((5,)),
            dma((5,)),
            dma((8,)),
            dma((8,)),
            dma((16,)),
            dma((16,)),
            dma((2,)),
            dma((2,)),
            dma((2,)),
            dma((2,)),
            dma((2,)),
            dma((2,)),
            dma((3,)),
            dma((3,)),
            pltpu.SemaphoreType.REGULAR,
            pltpu.SemaphoreType.REGULAR((3,)),
        ],
        compiler_params=pltpu.CompilerParams(
            collective_id=0, has_side_effects=True, vmem_limit_bytes=60 << 20
        ),
    )(attention, encoder_skip, depth_filter, point_weight, crop_offset, target_bins, cotangent)
    return pl.pallas_call(
        finish,
        out_shape=tuple(jax.ShapeDtypeStruct(o.shape, o.dtype) for o in outs),
        in_specs=[HBM] * 4,
        out_specs=(HBM,) * 4,
        scratch_shapes=[pltpu.VMEM(o.shape, o.dtype) for o in outs] + [dma((6,)), dma((6,))],
        compiler_params=pltpu.CompilerParams(vmem_limit_bytes=60 << 20),
    )(*outs)


def solution(mesh):
    in_specs = (
        P(None, "seq", "head"),
        P("head", "seq", None),
        P(),
        P("head", None),
        P("head"),
        P("head", None),
        P("head", "seq", None),
    )
    out_specs = (P("head", "seq", None), P("head", "seq", None), P("head", "seq", None), P())
    return jax.shard_map(shards, mesh=mesh, in_specs=in_specs, out_specs=out_specs, check_vma=False)
```

```python
import math

import jax
import jax.numpy as jnp
from jax import lax
from jax.experimental import pallas as pl
from jax.experimental.pallas import tpu as pltpu
from jax.sharding import PartitionSpec as P

MESH = pl.DeviceIdType.MESH
HBM = pl.BlockSpec(memory_space=pltpu.HBM)
VM = pl.BlockSpec(memory_space=pltpu.VMEM)
F32 = jnp.float32
BF16 = jnp.bfloat16

D = 1536
HEADS = 8
SEQ = 64
KD = D // HEADS
ROWS = 128
HALF = 64
LOCAL = 2
TILE = 128
OWNERS = D // TILE
PLANE = 32
ZS = 16
PAD = 8
BYY = False
ZL = 2
COT = 0
ATT = 2
Z_SIDES = ((1, -1), (-1, 1), (1, -1), (-1, -1), (1, 1), (-1, -1))
SCALE = 1.0 / math.sqrt(131072.0)


def dot(a, b):
    return jnp.dot(a, b, preferred_element_type=F32)


def dot_t(a, b):
    return lax.dot_general(a, b, (((1,), (1,)), ((), ())), preferred_element_type=F32)


def kernel(
    att,
    skip,
    filt_h,
    weight,
    offset_h,
    bins_h,
    cot,
    tgt_out,
    att_h,
    skip_h,
    filt_out,
    filt,
    offset,
    bins,
    attv,
    apack,
    attbuf,
    skipbuf,
    wbuf,
    cotbuf,
    summed,
    slope,
    gout,
    conv,
    edge_s,
    edge_r,
    edge2_s,
    edge2_r,
    rows_s,
    rows_r,
    terms,
    plane_r,
    zsum,
    z_r,
    final,
    fin_r,
    sbf,
    abf,
    pair,
    att_out,
    skip_out,
    local_sem,
    att_ss,
    att_rs,
    wx_ss,
    wx_rs,
    wy_ss,
    wy_rs,
    wz_ss,
    wz_rs,
    wc_ss,
    wc_rs,
    cot_sem,
    edge_ss,
    edge_rs,
    edge2_ss,
    edge2_rs,
    rows_sem,
    red_ss,
    red_rs,
    plane_in,
    z_in,
):
    s, h = lax.axis_index("seq"), lax.axis_index("head")
    z, xh, c = s // 4, (s // 2) % 2, s % 2
    xl, y = h // 4, h % 4
    x = 2 * xh + xl
    zp = z % 2

    def at(z_, xh_, c_, xl_, y_):
        return ((z_ * 2 + xh_) * 2 + c_, xl_ * 4 + y_)

    def x_peer(by):
        other = (x + by + 4) % 4
        return at(z, other // 2, c, other % 2, y)

    def y_peer(by):
        return (s, xl * 4 + (y + by + 8) % 4)

    def z_peer(by):
        return at((z + by + 2 * ZS) % ZS, xh, c, xl, y)

    core_peer = at(z, xh, 1 - c, xl, y)
    next_dev = ((s + 1) % SEQ, h)
    prev_dev = ((s + SEQ - 1) % SEQ, h)

    def plane_dev(r):
        return at(z, (r // 8) % 2, r // 16, (r // 4) % 2, r % 4)

    my_plane = c * 16 + xh * 8 + xl * 4 + y

    def owner(t):
        return t + 16 * (t % 2)

    own_w = pltpu.make_async_copy(weight, wbuf.at[pl.ds(h * KD, KD)], local_sem.at[0])
    own_skip = pltpu.make_async_copy(skip, skipbuf, local_sem.at[1])
    own_cot = pltpu.make_async_copy(cot, cotbuf.at[:, pl.ds(ROWS, ROWS)], local_sem.at[2])
    own_att = pltpu.make_async_copy(att, attv, local_sem.at[3])
    small = [
        pltpu.make_async_copy(filt_h, filt, local_sem.at[4]),
        pltpu.make_async_copy(offset_h, offset, local_sem.at[5]),
        pltpu.make_async_copy(bins_h, bins, local_sem.at[6]),
    ]
    own_att.start()
    own_w.start()
    for cp in small:
        cp.start()
    own_skip.start()
    own_cot.start()

    barrier = pltpu.get_barrier_semaphore()

    @pl.loop(1, HEADS)
    def _(i):
        pl.semaphore_signal(barrier, inc=1, device_id=(s, (h + i) % HEADS), device_id_type=MESH)

    quad = [at(z, 1 - xh, c, xl, y), core_peer, at(z, 1 - xh, 1 - c, xl, y)]
    near = quad + [x_peer(1), x_peer(-1), z_peer(1), z_peer(-1), next_dev, prev_dev]
    for dev in near:
        pl.semaphore_signal(barrier, inc=1, device_id=dev, device_id_type=MESH)
    own_att.wait()
    for i in range(HEADS):
        apack[i] = jnp.concatenate([attv[LOCAL * i], attv[LOCAL * i + 1]], axis=1)
    attbuf[h] = apack[h]
    pl.semaphore_wait(barrier, HEADS - 1 + len(near))

    def greet(sem, dev):
        pl.semaphore_signal(sem, inc=1, device_id=dev, device_id_type=MESH)

    for dev in quad:
        greet(plane_in, dev)
    for by in (1, -1):
        greet(z_in.at[0], z_peer(by))

    def remote(src, dst, ss, rs, dev):
        return pltpu.make_async_remote_copy(
            src_ref=src, dst_ref=dst, send_sem=ss, recv_sem=rs, device_id=dev, device_id_type=MESH
        )

    att_copies = []

    def start_att():
        for i in range(1, HEADS):
            to = (h + i) % HEADS
            cp = remote(
                apack.at[to], attbuf.at[h], att_ss.at[i - 1], att_rs.at[i - 1], (s, to)
            )
            cp.start()
            att_copies.append(cp)

    cot_copy = remote(cotbuf.at[:, pl.ds(ROWS, ROWS)], cotbuf.at[:, pl.ds(0, ROWS)], cot_sem.at[0], cot_sem.at[1], next_dev)

    quarter = KD // 4

    def piece(xl_, d, p, lo=0, n=KD // 4):
        row = (xl_ * 4 + (y + d) % 4) * KD + c * (KD // 2) + p * quarter + lo
        return wbuf.at[pl.ds(pl.multiple_of(row, 16), n)]

    own_w.wait()
    own_cot.wait()
    own = piece(xl, 0, zp)
    wy, wx, wz, core_copies, sent = {}, {}, [], [], []

    def send(src, dst, ss, rs, k, dev):
        cp = remote(src, dst, ss.at[k], rs.at[k], dev)
        cp.start()
        sent.append(cp)
        return cp

    def to_core(ref):
        k = len(core_copies)
        core_copies.append(send(ref, ref, wc_ss, wc_rs, k, core_peer))

    WHOLE, BIG, SMALL = (0, KD // 4), (0, 32), (32, 16)

    def to_x(k, side, d, part, src=None):
        dst = piece(xl, d, zp, *part)
        wx[k] = (send(dst if src is None else src, dst, wx_ss, wx_rs, k, x_peer(side)), d, part)

    busy = (0, xh, 1 - xh)[ZL]
    pair_side = 1 - 2 * xl

    def to_z(other, d, part=WHOLE):
        k = len(wz)
        calm, full = Z_SIDES[k]
        side = calm + busy * (full - calm)
        ref = piece(1 - xl if other else xl, d, zp, *part)
        wz.append((send(ref, ref, wz_ss, wz_rs, k, z_peer(side)), other, d, part))

    own_second = piece(xl, 0, 1 - zp)

    def second_y():
        for k, d in ((3, 1), (4, 3)):
            wy[k] = send(own_second, piece(xl, 0, 1 - zp), wy_ss, wy_rs, k, y_peer(-d))

    def to_y(k, other, d):
        dst = piece(1 - xl if other else xl, 0, zp)
        wy[k] = send(dst if other else own, dst, wy_ss, wy_rs, k, y_peer(-d))

    if ATT == 0:
        start_att()
    to_x(0, -pair_side, 0, WHOLE, own)
    to_y(0, False, 1)
    to_y(1, False, 3)
    if COT == 0:
        cot_copy.start()
    if ATT == 1:
        start_att()
    to_y(2, False, 2)
    if ATT == 3:
        second_y()
    if ATT == 2 or ATT == 3:
        start_att()
    if ATT != 3:
        second_y()
    if COT == 1:
        cot_copy.start()

    pl.semaphore_wait(z_in.at[0], 2)
    for by in (2, -2):
        greet(z_in.at[1], z_peer(by))

    def from_y(k, d):
        wy[k].wait_recv()
        if d == 2:
            to_z(False, d)
        to_core(piece(xl, d, zp))

    def from_x(k):
        cp, d, part = wx[k]
        cp.wait_recv()
        to_z(True, d, part)
        to_core(piece(1 - xl, d, zp, *part))

    def stage1():
        from_y(0, 1)
        if not BYY:
            to_x(1, pair_side, 1, WHOLE)
        from_y(1, 3)
        if not BYY:
            to_x(2, -pair_side, 3, WHOLE)
        from_x(0)
        if BYY:
            to_y(3, True, 1)
            to_y(4, True, 3)
        if COT == 2:
            cot_copy.start()

    def stage2():
        from_y(2, 2)
        to_x(3, pair_side if BYY else -pair_side, 2, BIG)
        to_x(4, -pair_side if BYY else pair_side, 2, SMALL)
        if COT == 3:
            cot_copy.start()

    def stage3(i):
        if BYY:
            wy[3 + i].wait_recv()
            to_z(True, 1 + 2 * i)
            to_core(piece(1 - xl, 1 + 2 * i, zp))
        else:
            from_x(1 + i)

    def stage4():
        from_x(3)
        from_x(4)

    for cp in small:
        cp.wait()
    own_skip.wait()
    stage1()
    stage2()
    pl.semaphore_wait(z_in.at[1], 2)
    for by in (4, -4):
        greet(z_in.at[2], z_peer(by))
    for cp in att_copies:
        cp.wait_recv()
    up = (
        lax.broadcasted_iota(jnp.int32, (ROWS, HALF), 0) // 2
        == lax.broadcasted_iota(jnp.int32, (ROWS, HALF), 1)
    ).astype(BF16)
    for b in range(LOCAL):
        for k in range(HEADS // 2):
            lane = slice(b * KD, (b + 1) * KD)
            wide = jnp.concatenate([dot(up, attbuf[2 * k])[:, lane], dot(up, attbuf[2 * k + 1])[:, lane]], axis=1)
            cols = pl.ds(2 * KD * k, 2 * KD)
            both = (wide + skipbuf[b, :, cols].astype(F32)).astype(BF16)
            sbf[pl.ds(b * ROWS, ROWS), cols] = both
            summed[b, pl.ds(PAD, ROWS), cols] = both.astype(F32)
        summed[b, pl.ds(PAD - 1, 1), :] = jnp.zeros((1, D), F32)
        summed[b, pl.ds(PAD + ROWS, 1), :] = jnp.zeros((1, D), F32)
        edge_s[0, pl.ds(b, 1), :] = summed[b, pl.ds(PAD, 1), :]
        edge_s[1, pl.ds(b, 1), :] = summed[b, pl.ds(PAD + ROWS - 1, 1), :]
    edges = [
        remote(edge_s.at[0], edge_r.at[1], edge_ss.at[0], edge_rs.at[1], prev_dev),
        remote(edge_s.at[1], edge_r.at[0], edge_ss.at[1], edge_rs.at[0], next_dev),
    ]
    for cp in edges:
        cp.start()

    def forward(b, low, n, part=0, parts=1):
        @pl.loop(part * D // TILE // parts, (part + 1) * D // TILE // parts)
        def _(t):
            cols = pl.ds(pl.multiple_of(t * TILE, TILE), TILE)
            taps = filt[:, cols]
            v = (
                taps[0:1] * summed[b, pl.ds(PAD - 1 + low, n), cols]
                + taps[1:2] * summed[b, pl.ds(PAD + low, n), cols]
                + taps[2:3] * summed[b, pl.ds(PAD + 1 + low, n), cols]
            )
            phi = 0.5 * (1.0 + lax.erf(v * 0.7071067811865476))
            abf[pl.ds(b * ROWS + low, n), cols] = (v * phi).astype(BF16)
            slope[b, pl.ds(low, n), cols] = phi + v * jnp.exp(-0.5 * v * v) * 0.3989422804014327

    forward(0, 0, ROWS, 0, 2)
    stage3(0)
    stage3(1)
    forward(0, 0, ROWS, 1, 2)
    stage4()
    forward(1, 0, ROWS)
    for cp in edges:
        cp.wait_recv()
    first, last = (s > 0).astype(F32), (s < SEQ - 1).astype(F32)
    for b in range(LOCAL):
        summed[b, pl.ds(PAD - 1, 1), :] = edge_r[0, pl.ds(b, 1), :] * first
        summed[b, pl.ds(PAD + ROWS, 1), :] = edge_r[1, pl.ds(b, 1), :] * last

    for b in range(LOCAL):
        forward(b, 0, 16)
        forward(b, ROWS - 16, 16)

    cot_copy.wait()
    place = lax.broadcasted_iota(jnp.int32, (ROWS, 2 * ROWS), 1)
    row = lax.broadcasted_iota(jnp.int32, (ROWS, 2 * ROWS), 0)
    for b in range(LOCAL):
        chosen = (place == row + (ROWS - offset[b])) & ((place >= ROWS) | (s > 0))
        moved = dot(chosen.astype(BF16), cotbuf[b])
        gout[pl.ds(b * ROWS, ROWS), :] = moved.astype(BF16)

    pick = lax.broadcasted_iota(jnp.int32, (16, LOCAL * ROWS), 0)
    spot = lax.broadcasted_iota(jnp.int32, (16, LOCAL * ROWS), 1)
    hit = jnp.zeros((16, LOCAL * ROWS), jnp.bool_)
    before = jnp.maximum(s - 1, 0)
    for b in range(LOCAL):
        for j in range(2):
            mine = bins[b, 2 * s + j] + offset[b]
            theirs = bins[b, 2 * before + j] + offset[b] - ROWS
            hit = hit | (
                (pick == 2 * b + j) & (spot == mine + b * ROWS) & (spot < (b + 1) * ROWS)
            )
            hit = hit | (
                (pick == 4 + 2 * b + j) & (spot == theirs + b * ROWS) & (spot >= b * ROWS) & (s > 0)
            )
    hit = hit.astype(BF16)
    act_rows = dot(hit, abf[...]).astype(BF16)
    sum_rows = dot(hit, sbf[...])

    pl.semaphore_wait(plane_in, 3)
    pl.semaphore_wait(z_in.at[2], 2)

    def block(pair_at):
        start = pl.multiple_of(pair_at * 2 * KD, TILE)
        cols = pl.ds(start, 2 * KD)
        ga = dot_t(gout[...], wbuf[cols, :])
        sums = [0.0, 0.0, 0.0]
        for b in range(LOCAL):
            gc = (ga[b * ROWS : (b + 1) * ROWS] * slope[b, :, cols]).astype(BF16).astype(F32)
            conv[b, pl.ds(PAD, ROWS), cols] = gc
            for k in range(3):
                sums[k] = sums[k] + jnp.sum(
                    gc * summed[b, pl.ds(PAD - 1 + k, ROWS), cols], axis=0, keepdims=True
                )
        for u in range(3):
            t = 3 * pair_at + u
            for k in range(3):
                terms[t, pl.ds(k, 1), :] = sums[k][:, u * TILE : (u + 1) * TILE]
            terms[t, pl.ds(3, 1), :] = jnp.zeros((1, TILE), F32)
            to = owner(t)

            @pl.when(my_plane != to)
            def _():
                remote(terms.at[t], plane_r.at[my_plane], red_ss.at[0], red_rs.at[0], plane_dev(to)).start()

            @pl.when(my_plane == to)
            def _():
                plane_r[my_plane] = terms[t]

    def from_z(*which):
        for k in which:
            cp, other, d, part = wz[k]
            cp.wait_recv()
            to_core(piece(1 - xl if other else xl, d, 1 - zp, *part))

    def from_core(*which):
        for k in which:
            core_copies[k].wait_recv()

    yh = y // 2
    for k, d in ((3, 1), (4, 3)):
        wy[k].wait_recv()
        to_core(piece(xl, d, 1 - zp))
    from_z(0, 1)
    from_core(0, 1, 8, 9)
    block(2 * xl + yh)
    from_z(2, 3)
    from_core(3, 11)
    block(2 * xl + 1 - yh)
    from_z(4, 5)
    from_core(2, 4, 5, 10, 12, 13)
    block(2 * (1 - xl) + yh)
    from_core(6, 7, 14, 15)
    block(2 * (1 - xl) + 1 - yh)
    for b in range(LOCAL):
        edge2_s[0, pl.ds(b, 1), :] = conv[b, pl.ds(PAD, 1), :]
        edge2_s[1, pl.ds(b, 1), :] = conv[b, pl.ds(PAD + ROWS - 1, 1), :]

    edges2 = [
        remote(edge2_s.at[0], edge2_r.at[1], edge2_ss.at[0], edge2_rs.at[1], prev_dev),
        remote(edge2_s.at[1], edge2_r.at[0], edge2_ss.at[1], edge2_rs.at[0], next_dev),
    ]
    for cp in edges2:
        cp.start()

    block_rows = (sum_rows + dot(act_rows, wbuf[...])).astype(BF16).astype(F32)
    rows_s[...] = block_rows[0:8]
    rows_copy = remote(rows_s.at[pl.ds(4, 4)], rows_r, rows_sem.at[0], rows_sem.at[1], prev_dev)

    far_first = sorted(
        [(dx, dy, dc) for dx in range(4) for dy in range(4) for dc in range(2) if dx or dy or dc],
        key=lambda o: -(min(o[0], 4 - o[0]) + min(o[1], 4 - o[1])),
    )
    t_mine = my_plane % 16
    owns = (t_mine < OWNERS) & (my_plane // 16 == t_mine % 2)

    @pl.when(owns)
    def _():
        part = plane_r.at[pl.ds(0, PLANE - 1)]
        pltpu.make_async_copy(part, part, red_rs.at[0]).wait()
        total = plane_r[0]
        for i in range(1, PLANE):
            total = total + plane_r[i]
        zsum[...] = total
        z_r[z] = total
        for i in sorted(range(1, ZS), key=lambda i: -min(i, ZS - i)):
            remote(zsum, z_r.at[z], red_ss.at[1], red_rs.at[1], z_peer(i)).start()

    rows_copy.start()

    for cp in edges2:
        cp.wait()
    for b in range(LOCAL):
        conv[b, pl.ds(PAD - 1, 1), :] = edge2_r[0, pl.ds(b, 1), :] * first
        conv[b, pl.ds(PAD + ROWS, 1), :] = edge2_r[1, pl.ds(b, 1), :] * last
    out_copies = []
    for b in range(LOCAL):

        @pl.loop(0, D // TILE)
        def _(t):
            cols = pl.ds(pl.multiple_of(t * TILE, TILE), TILE)
            taps = filt[:, cols]
            gs = (
                gout[pl.ds(b * ROWS, ROWS), cols].astype(F32)
                + taps[0:1] * conv[b, pl.ds(PAD + 1, ROWS), cols]
                + taps[1:2] * conv[b, pl.ds(PAD, ROWS), cols]
                + taps[2:3] * conv[b, pl.ds(PAD - 1, ROWS), cols]
            )
            skip_out[b, :, cols] = gs.astype(BF16)
            pair[...] = gs
            att_out[b, :, cols] = (
                pair[pl.ds(0, HALF, stride=2), :] + pair[pl.ds(1, HALF, stride=2), :]
            ).astype(BF16)

        for i, (src, dst) in enumerate(((skip_out, skip_h), (att_out, att_h))):
            cp = pltpu.make_async_copy(src.at[b], dst.at[b], local_sem.at[7 + 2 * b + i])
            cp.start()
            out_copies.append(cp)

    rows_copy.wait()
    for b in range(LOCAL):
        whole = rows_s[pl.ds(2 * b, 2), :] + rows_r[pl.ds(2 * b, 2), :] * last
        tgt_out[b] = whole.astype(BF16)

    for cp in out_copies:
        cp.wait()
    for cp in att_copies + sent + edges:
        cp.wait_send()

    @pl.when(owns)
    def _():
        part = plane_r.at[pl.ds(0, OWNERS - 1)]
        pltpu.make_async_copy(part, part, red_ss.at[0]).wait()
        part = z_r.at[pl.ds(0, ZS - 1)]
        pltpu.make_async_copy(part, part, red_ss.at[1]).wait()

    @pl.when(jnp.logical_not(owns))
    def _():
        part = plane_r.at[pl.ds(0, OWNERS)]
        pltpu.make_async_copy(part, part, red_ss.at[0]).wait()

    @pl.when(owns)
    def _():
        part = z_r.at[pl.ds(0, ZS - 1)]
        pltpu.make_async_copy(part, part, red_rs.at[1]).wait()
        total = z_r[0]
        for i in range(1, ZS):
            total = total + z_r[i]
        final[...] = total * SCALE
        fin_r[t_mine] = total * SCALE

        for dx, dy, dc in far_first:
            other = (x + dx) % 4
            to = at(z, other // 2, 1 - c if dc else c, other % 2, (y + dy) % 4)
            remote(final, fin_r.at[t_mine], red_ss.at[2], red_rs.at[2], to).start()

    @pl.when(owns)
    def _():
        part = fin_r.at[pl.ds(0, OWNERS - 1)]
        pltpu.make_async_copy(part, part, red_rs.at[2]).wait()

    @pl.when(jnp.logical_not(owns))
    def _():
        pltpu.make_async_copy(fin_r, fin_r, red_rs.at[2]).wait()

    for t in range(OWNERS):
        filt_out[:, pl.ds(t * TILE, TILE)] = fin_r[t, pl.ds(0, 3), :]

    @pl.when(owns)
    def _():
        part = plane_r.at[pl.ds(0, PLANE - 1)]
        pltpu.make_async_copy(part, part, red_ss.at[2]).wait()


def finish(a, b, c, d, a_out, b_out, c_out, d_out, av, bv, cv, dv, sem_in, sem_out):
    parts = [(c.at[i], cv.at[i], c_out.at[i]) for i in range(LOCAL)]
    parts += [(b.at[i], bv.at[i], b_out.at[i]) for i in range(LOCAL)]
    parts += [(d, dv, d_out), (a, av, a_out)]
    ins = [pltpu.make_async_copy(x, v, sem_in.at[i]) for i, (x, v, _) in enumerate(parts)]
    outs = [pltpu.make_async_copy(v, o, sem_out.at[i]) for i, (_, v, o) in enumerate(parts)]
    for cp in ins:
        cp.start()
    for cp_in, cp_out in zip(ins, outs):
        cp_in.wait()
        cp_out.start()
    for cp in outs:
        cp.wait()


def shards(attention, encoder_skip, depth_filter, point_weight, crop_offset, target_bins, cotangent):
    dma = pltpu.SemaphoreType.DMA
    wide = ROWS + 2 * PAD
    outs = pl.pallas_call(
        kernel,
        out_shape=(
            jax.ShapeDtypeStruct((LOCAL, 2, D), BF16),
            jax.ShapeDtypeStruct((LOCAL, HALF, D), BF16),
            jax.ShapeDtypeStruct((LOCAL, ROWS, D), BF16),
            jax.ShapeDtypeStruct((3, D), F32),
        ),
        in_specs=[HBM] * 7,
        out_specs=(VM, HBM, HBM, VM),
        scratch_shapes=[
            pltpu.VMEM((3, D), F32),
            pltpu.SMEM((LOCAL,), jnp.int32),
            pltpu.SMEM((LOCAL, 128), jnp.int32),
            pltpu.VMEM((LOCAL * HEADS, HALF, KD), BF16),
            pltpu.VMEM((HEADS, HALF, LOCAL * KD), BF16),
            pltpu.VMEM((HEADS, HALF, LOCAL * KD), BF16),
            pltpu.VMEM((LOCAL, ROWS, D), BF16),
            pltpu.VMEM((D, D), BF16),
            pltpu.VMEM((LOCAL, 2 * ROWS, D), BF16),
            pltpu.VMEM((LOCAL, wide, D), F32),
            pltpu.VMEM((LOCAL, ROWS, D), F32),
            pltpu.VMEM((LOCAL * ROWS, D), BF16),
            pltpu.VMEM((LOCAL, wide, D), F32),
            pltpu.VMEM((2, LOCAL, D), F32),
            pltpu.VMEM((2, LOCAL, D), F32),
            pltpu.VMEM((2, LOCAL, D), F32),
            pltpu.VMEM((2, LOCAL, D), F32),
            pltpu.VMEM((8, D), F32),
            pltpu.VMEM((4, D), F32),
            pltpu.VMEM((OWNERS, 4, TILE), F32),
            pltpu.VMEM((PLANE, 4, TILE), F32),
            pltpu.VMEM((4, TILE), F32),
            pltpu.VMEM((ZS, 4, TILE), F32),
            pltpu.VMEM((4, TILE), F32),
            pltpu.VMEM((OWNERS, 4, TILE), F32),
            pltpu.VMEM((LOCAL * ROWS, D), BF16),
            pltpu.VMEM((LOCAL * ROWS, D), BF16),
            pltpu.VMEM((ROWS, TILE), F32),
            pltpu.VMEM((LOCAL, HALF, D), BF16),
            pltpu.VMEM((LOCAL, ROWS, D), BF16),
            dma((11,)),
            dma((HEADS - 1,)),
            dma((HEADS - 1,)),
            dma((5,)),
            dma((5,)),
            dma((5,)),
            dma((5,)),
            dma((8,)),
            dma((8,)),
            dma((16,)),
            dma((16,)),
            dma((2,)),
            dma((2,)),
            dma((2,)),
            dma((2,)),
            dma((2,)),
            dma((2,)),
            dma((3,)),
            dma((3,)),
            pltpu.SemaphoreType.REGULAR,
            pltpu.SemaphoreType.REGULAR((3,)),
        ],
        compiler_params=pltpu.CompilerParams(
            collective_id=0, has_side_effects=True, vmem_limit_bytes=60 << 20
        ),
    )(attention, encoder_skip, depth_filter, point_weight, crop_offset, target_bins, cotangent)
    return pl.pallas_call(
        finish,
        out_shape=tuple(jax.ShapeDtypeStruct(o.shape, o.dtype) for o in outs),
        in_specs=[HBM] * 4,
        out_specs=(HBM,) * 4,
        scratch_shapes=[pltpu.VMEM(o.shape, o.dtype) for o in outs] + [dma((6,)), dma((6,))],
        compiler_params=pltpu.CompilerParams(vmem_limit_bytes=60 << 20),
    )(*outs)


def solution(mesh):
    in_specs = (
        P(None, "seq", "head"),
        P("head", "seq", None),
        P(),
        P("head", None),
        P("head"),
        P("head", None),
        P("head", "seq", None),
    )
    out_specs = (P("head", "seq", None), P("head", "seq", None), P("head", "seq", None), P())
    return jax.shard_map(shards, mesh=mesh, in_specs=in_specs, out_specs=out_specs, check_vma=False)
```
